256 devices in a mesh: ta: 32 (over y, z), gx: 8 (over x, core).
Axes of the slice: x: 4, y: 4, z: 8, core: 2. Of those that a mesh axis runs over, the one named last changes fastest.
Arguments:
- right_side: float32 [256, 64, 64, 128], P('ta', 'gx'), may hold values from -6 to 6
- basis_x: float32 [64, 64], replicated, may hold values from -0.75 to 0.75
- basis_y: float32 [64, 64], replicated, may hold values from -0.75 to 0.75
- basis_z: float32 [128, 128], replicated, may hold values from -0.5 to 0.5
- eig_x: float32 [64], replicated, may hold values from 4 to 21.3248
- eig_y: float32 [64], replicated, may hold values from 4 to 21.3248
- eig_z: float32 [128], replicated, may hold values from 4 to 21.3248
- steps: float32 [256], replicated, may hold values from 0.25 to 1
Outputs:
- preconditioned: float32 [256, 64, 64, 128], P('ta', 'gx')
The draws below stay inside these ranges and needn't reach their ends.
All inputs are finite; a program needn't handle non-finite values.
Results may differ from the reference program's by a relative error of at most 0.00012.
Values sent between devices are 32-bit elements; how exact they have to be, the bound alone decides.
No kernel may reach another device: no remote copies, remote signals or barrier semaphores. Data moves between devices by JAX's collectives and lax.ppermute only.
A program may use at most 192 MiB of HBM per device.

```python
import math
import jax
import jax.numpy as jnp
from jax import lax

NX = 64
NY = 64
NZ = 128
NT = 256


def steps_of(own_key, extent, split, low, largest):
    gain, own = 1.0, jax.random.fold_in(own_key, 6)
    for axis_at, blocks in split:
        draws = jnp.exp(jax.random.uniform(jax.random.fold_in(own, axis_at), (blocks,), jnp.float32, low / len(split), largest / len(split)))
        gain = gain * jnp.repeat(draws, extent[axis_at] // blocks).reshape([-1 if axis == axis_at else 1 for axis in range(len(extent))])
    return gain


def noise(key, dims, deviation, most, shards=(), held_as=jnp.bfloat16):
    drawn = jax.random.normal(key, dims, jnp.float32) * deviation
    if len(shards) > 0:
        drawn = steps_of(key, dims, shards, -0.22, 0.18) * drawn
    return jnp.clip(drawn, min=-most, max=most).astype(held_as)


def setup_inputs(seed: int = 0) -> dict:
    key_of = jax.random.split(jax.random.key(seed), 9)
    return {
        "right_side": noise(key_of[0], (NT, NX, NY, NZ), 1.0, 6.0, ((0, 32), (1, 8)), jnp.float32),
        "basis_x": noise(key_of[1], (NX, NX), NX ** -0.5, 0.75, (), jnp.float32),
        "basis_y": noise(key_of[2], (NY, NY), NY ** -0.5, 0.75, (), jnp.float32),
        "basis_z": noise(key_of[3], (NZ, NZ), NZ ** -0.5, 0.5, (), jnp.float32),
        "eig_x": jnp.clip(jnp.exp(jax.random.uniform(key_of[4], (NX,), jnp.float32, math.log(4.0), math.log(21.3248))), 4.0, 21.3248),
        "eig_y": jnp.clip(jnp.exp(jax.random.uniform(key_of[5], (NY,), jnp.float32, math.log(4.0), math.log(21.3248))), 4.0, 21.3248),
        "eig_z": jnp.clip(jnp.exp(jax.random.uniform(key_of[6], (NZ,), jnp.float32, math.log(4.0), math.log(21.3248))), 4.0, 21.3248),
        "steps": jnp.clip(jnp.exp(jax.random.uniform(key_of[7], (NT,), jnp.float32, math.log(0.25), math.log(1.0))), 0.25, 1.0),
    }


precise = lax.Precision.HIGHEST

def reference(right_side, basis_x, basis_y, basis_z, eig_x, eig_y, eig_z, steps):

    def forward(time_plane):
        halfway = jnp.einsum('abc,cl->abl', time_plane, basis_z, precision=precise)
        halfway = jnp.einsum('abc,bj->ajc', halfway, basis_y, precision=precise)
        return jnp.einsum('abc,ai->ibc', halfway, basis_x, precision=precise)
    spectral = lax.map(forward, right_side)
    total_rows = steps.shape[0]
    lengths = steps / total_rows
    following = jnp.concatenate([lengths[1:], jnp.zeros((1,), lengths.dtype)])
    position = jnp.arange(total_rows, dtype=jnp.int32)
    closing = jnp.where(position == total_rows - 1, 0.5, 0.0).astype(lengths.dtype)

    def solve_slab(mode_at):
        time_rows = lax.dynamic_index_in_dim(spectral, mode_at, 1, keepdims=False)
        eigen_sum = (eig_x[mode_at] + eig_y[:, None] + eig_z[None, :])[:, :, None]
        sub_diag = jnp.where(position == 0, 0.0, eigen_sum * (lengths / 6.0) - 0.5)
        main_diag = eigen_sum * ((lengths + following) / 3.0) + closing
        super_diag = jnp.where(position == total_rows - 1, 0.0, eigen_sum * (following / 6.0) + 0.5)
        right_rows = jnp.transpose(time_rows, (1, 2, 0))[..., None]
        result = lax.linalg.tridiagonal_solve(sub_diag, main_diag, super_diag, right_rows)[..., 0]
        return jnp.transpose(result, (2, 0, 1))
    solved = lax.map(solve_slab, jnp.arange(NX, dtype=jnp.int32))

    def backward(time_at):
        time_plane = lax.dynamic_index_in_dim(solved, time_at, 1, keepdims=False)
        halfway = jnp.einsum('ibc,ai->abc', time_plane, basis_x, precision=precise)
        halfway = jnp.einsum('ajl,cl->ajc', halfway, basis_z, precision=precise)
        return jnp.einsum('ajc,bj->abc', halfway, basis_y, precision=precise)
    return lax.map(backward, jnp.arange(total_rows, dtype=jnp.int32))
```

```python
from functools import partial

import jax
import jax.numpy as jnp
from jax import lax
from jax.experimental import pallas as pl
from jax.experimental.pallas import tpu as pltpu
from jax.sharding import PartitionSpec as P

f32, bf16 = jnp.float32, jnp.bfloat16
params = partial(pltpu.CompilerParams, vmem_limit_bytes=48 * 2**20)


def split(x):
    high = x.astype(bf16)
    return high, (x - high.astype(f32)).astype(bf16)


def dot3(left, right):
    (lh, ll), (rh, rl) = left, right
    mm = partial(jnp.dot, preferred_element_type=f32)
    return mm(lh, rh) + (mm(lh, rl) + mm(ll, rh))


def cost(flops, bytes_accessed):
    return pl.CostEstimate(flops=int(flops), bytes_accessed=int(bytes_accessed), transcendentals=0)


def forward_body(x_ref, by_ref, bz_ref, out_ref):
    rows, y, z = x_ref.shape[1:]
    vol = dot3(split(x_ref[0].reshape(rows * y, z)), split(bz_ref[...]))
    by = split(by_ref[...])
    for a in range(rows):
        plane = dot3(by, split(vol[a * y : (a + 1) * y]))
        out_ref[:, 0, a] = plane.reshape(out_ref.shape[0], y // out_ref.shape[0], z)


def forward_yz(x, by_t, bz, members):
    t, a, y, z = x.shape
    span = y // members
    return pl.pallas_call(
        forward_body,
        grid=(t,),
        in_specs=[
            pl.BlockSpec((1, a, y, z), lambda k: (k, 0, 0, 0)),
            pl.BlockSpec((y, y), lambda k: (0, 0)),
            pl.BlockSpec((z, z), lambda k: (0, 0)),
        ],
        out_specs=pl.BlockSpec((members, 1, a, span, z), lambda k: (0, k, 0, 0, 0)),
        out_shape=jax.ShapeDtypeStruct((members, t, a, span, z), f32),
        compiler_params=params(),
        cost_estimate=cost(6 * t * a * y * z * (y + z), 8 * x.size),
        name="forward_yz",
    )(x, by_t, bz)


def backward_body(x_ref, by_ref, bz_ref, out_ref):
    rows, y, z = out_ref.shape[1:]
    by, bz = split(by_ref[...]), split(bz_ref[...])
    planes = [
        dot3(by, split(x_ref[:, 0, a].reshape(y, z))) for a in range(rows)
    ]
    vol = jnp.concatenate(planes, axis=0)
    out_ref[0] = dot3(split(vol), bz).reshape(rows, y, z)


def backward_yz(x, by, bz_t):
    members, t, a, span, z = x.shape
    y = members * span
    return pl.pallas_call(
        backward_body,
        grid=(t,),
        in_specs=[
            pl.BlockSpec((members, 1, a, span, z), lambda k: (0, k, 0, 0, 0)),
            pl.BlockSpec((y, y), lambda k: (0, 0)),
            pl.BlockSpec((z, z), lambda k: (0, 0)),
        ],
        out_specs=pl.BlockSpec((1, a, y, z), lambda k: (k, 0, 0, 0)),
        out_shape=jax.ShapeDtypeStruct((t, a, y, z), f32),
        compiler_params=params(),
        cost_estimate=cost(6 * t * a * y * z * (y + z), 8 * x.size),
        name="backward_yz",
    )(x, by, bz_t)


def row_terms(eigen, lens, k, closing):
    main = eigen * ((lens[k] + lens[k + 1]) / 3.0) + closing
    sub = eigen * (lens[k] / 6.0) - 0.5
    sup = eigen * (lens[k + 1] / 6.0) + 0.5
    return main, sub, sup


def reduced_body(count, rows, lens_ref, eigen_ref, cl_ref, e_ref, a_ref, k_ref, b_ref, q_ref):
    eigen = eigen_ref[...]

    def block(j, carry):
        lens = [lens_ref[j * rows + k] for k in range(rows + 1)]
        pivots, subs, ratios = [], [], []
        for k in range(rows):
            closing = jnp.where(jnp.logical_and(j == count - 1, k == rows - 1), 0.5, 0.0)
            main, sub, sup = row_terms(eigen, lens, k, closing)
            pivot = main - sub * ratios[-1] if k else main
            inverse = 1.0 / pivot
            pivots.append(inverse)
            subs.append(sub)
            ratios.append(sup * inverse)
        front = subs[0] * pivots[0]
        fronts = [front]
        for k in range(1, rows):
            front = -(subs[k] * pivots[k]) * front
            fronts.append(front)
        last = ratios[rows - 1]
        low = fronts[rows - 1]
        cl_ref[j] = low
        e_ref[j] = last
        for k in reversed(range(rows - 1)):
            low = fronts[k] - ratios[k] * low
            last = -ratios[k] * last
        a_ref[j] = low
        b_ref[j] = last
        return carry

    lax.fori_loop(0, count, block, 0, unroll=4)

    def sweep(j, q_before):
        v_last, w_last, v_first, w_first = cl_ref[j], e_ref[j], a_ref[j], b_ref[j]
        scale = 1.0 / (1.0 - v_first * q_before)
        back = w_first * scale
        q_now = w_last + v_last * q_before * back
        e_now = v_last * scale
        cl_ref[j] = e_now * q_before
        e_ref[j] = e_now
        a_ref[j] = scale
        k_ref[j] = v_first * scale
        b_ref[j] = back
        q_ref[j] = q_now
        return q_now

    lax.fori_loop(0, count, sweep, jnp.zeros_like(eigen))


def reduced_terms(lens, eigen, count, rows):
    shape = (count,) + eigen.shape
    return pl.pallas_call(
        partial(reduced_body, count, rows),
        in_specs=[
            pl.BlockSpec(memory_space=pltpu.SMEM),
            pl.BlockSpec(memory_space=pltpu.VMEM),
        ],
        out_specs=[pl.BlockSpec(memory_space=pltpu.VMEM)] * 6,
        out_shape=[jax.ShapeDtypeStruct(shape, f32)] * 6,
        compiler_params=params(),
        cost_estimate=cost(40 * rows * count * eigen.size, 24 * count * eigen.size),
        name="reduced_terms",
    )(lens, eigen)


def interface_body(count, g_ref, cl_ref, e_ref, a_ref, k_ref, b_ref, q_ref, out_ref, fh_ref):
    zero = jnp.zeros(g_ref.shape[2:], f32)

    def down(j, before):
        first, last = g_ref[j, 0], g_ref[j, 1]
        out_ref[j, 0] = before
        fh_ref[j] = a_ref[j] * first - k_ref[j] * before
        return (last + cl_ref[j] * first) - e_ref[j] * before

    top = lax.fori_loop(0, count, down, zero, unroll=8)
    fh_ref[count] = top

    def up(i, after):
        j = count - 1 - i
        out_ref[j, 1] = after

        @pl.when(j < count - 1)
        def _():
            out_ref[j + 1, 0] = out_ref[j + 1, 0] - q_ref[j] * after

        return fh_ref[j] - b_ref[j] * after

    lax.fori_loop(0, count, up, zero, unroll=8)


def interface_solve(g, terms):
    count = g.shape[0]
    return pl.pallas_call(
        partial(interface_body, count),
        in_specs=[pl.BlockSpec(memory_space=pltpu.VMEM)] * 7,
        out_specs=pl.BlockSpec(memory_space=pltpu.VMEM),
        out_shape=jax.ShapeDtypeStruct(g.shape, f32),
        scratch_shapes=[pltpu.VMEM((count + 1,) + g.shape[2:], f32)],
        compiler_params=params(),
        cost_estimate=cost(6 * g.size, 20 * g.size),
        name="interface_solve",
    )(g, *terms)


def eliminate_body(lens_ref, close_ref, x_ref, eigen_ref, wh_ref, wl_ref, g_ref, ends_ref, ratio_ref):
    t = pl.program_id(0)
    rows, modes, lanes = g_ref.shape
    spectral = dot3((wh_ref[...], wl_ref[...]), split(x_ref[:, 0].reshape(modes, lanes)))
    eigen = eigen_ref[...]
    main = eigen * ((lens_ref[t] + lens_ref[t + 1]) / 3.0) + close_ref[t]
    sub = eigen * (lens_ref[t] / 6.0) - 0.5
    sup = eigen * (lens_ref[t + 1] / 6.0) + 0.5

    @pl.when(t == 0)
    def _():
        inverse = 1.0 / main
        ratio_ref[t] = sup * inverse
        g_ref[t] = spectral * inverse

    @pl.when(t > 0)
    def _():
        inverse = 1.0 / (main - sub * ratio_ref[t - 1])
        ratio_ref[t] = sup * inverse
        g_ref[t] = (spectral - sub * g_ref[t - 1]) * inverse

    @pl.when(t == rows - 1)
    def _():
        split_shape = (ends_ref.shape[0], modes // ends_ref.shape[0], lanes)
        now = g_ref[rows - 1]
        ends_ref[:, 1] = now.reshape(split_shape)
        for k in reversed(range(rows - 1)):
            now = g_ref[k] - ratio_ref[k] * now
            g_ref[k] = now
        ends_ref[:, 0] = now.reshape(split_shape)


def eliminate(x, eigen, weights, lens, close, count):
    members, t, a, span, z = x.shape
    modes = members * a * span
    whole = lambda *shape: pl.BlockSpec(shape, lambda k: (0,) * len(shape))
    return pl.pallas_call(
        eliminate_body,
        grid=(t,),
        in_specs=[
            pl.BlockSpec(memory_space=pltpu.SMEM),
            pl.BlockSpec(memory_space=pltpu.SMEM),
            pl.BlockSpec((members, 1, a, span, z), lambda k: (0, k, 0, 0, 0)),
            whole(modes, z),
            whole(modes, modes),
            whole(modes, modes),
        ],
        out_specs=[whole(t, modes, z), whole(count, 2, modes // count, z)],
        out_shape=[
            jax.ShapeDtypeStruct((t, modes, z), f32),
            jax.ShapeDtypeStruct((count, 2, modes // count, z), f32),
        ],
        scratch_shapes=[pltpu.VMEM((t, modes, z), f32)],
        compiler_params=params(),
        cost_estimate=cost(6 * t * modes * modes * z, 8 * x.size),
        name="eliminate",
    )(lens, close, x, eigen, *weights)


def substitute_body(lens_ref, close_ref, g_ref, ends_ref, eigen_ref, wh_ref, wl_ref, out_ref, sol_ref):
    t = pl.program_id(0)
    rows, modes, lanes = g_ref.shape

    @pl.when(t == 0)
    def _():
        eigen = eigen_ref[...]
        lens = [lens_ref[k] for k in range(rows + 1)]
        before = ends_ref[:, 0].reshape(modes, lanes)
        after = ends_ref[:, 1].reshape(modes, lanes)
        ratios, values = [], []
        for k in range(rows):
            main, sub, sup = row_terms(eigen, lens, k, close_ref[k])
            inverse = 1.0 / (main - sub * ratios[-1] if k else main)
            ratios.append(sup * inverse)
            value = -(sub * inverse) * (values[-1] if k else before)
            if k == rows - 1:
                value = value - ratios[-1] * after
            values.append(value)
        now = values[rows - 1]
        sol_ref[rows - 1] = g_ref[rows - 1] + now
        for k in reversed(range(rows - 1)):
            now = values[k] - ratios[k] * now
            sol_ref[k] = g_ref[k] + now

    cell = dot3((wh_ref[...], wl_ref[...]), split(sol_ref[t]))
    out_ref[:, 0] = cell.reshape(out_ref.shape[:1] + out_ref.shape[2:])


def substitute(g, ends, eigen, weights, lens, close, members):
    t, modes, z = g.shape
    span = 8
    a = modes // (members * span)
    whole = lambda *shape: pl.BlockSpec(shape, lambda k: (0,) * len(shape))
    return pl.pallas_call(
        substitute_body,
        grid=(t,),
        in_specs=[
            pl.BlockSpec(memory_space=pltpu.SMEM),
            pl.BlockSpec(memory_space=pltpu.SMEM),
            whole(t, modes, z),
            whole(*ends.shape),
            whole(modes, z),
            whole(modes, modes),
            whole(modes, modes),
        ],
        out_specs=pl.BlockSpec((members, 1, a, span, z), lambda k: (0, k, 0, 0, 0)),
        out_shape=jax.ShapeDtypeStruct((members, t, a, span, z), f32),
        scratch_shapes=[pltpu.VMEM((t, modes, z), f32)],
        compiler_params=params(),
        cost_estimate=cost(6 * t * modes * modes * z, 8 * g.size),
        name="substitute",
    )(lens, close, g, ends, eigen, *weights)


def spread_body(bx_ref, fh_ref, fl_ref, bh_ref, bl_ref):
    x = bx_ref.shape[0]
    modes = fh_ref.shape[0]
    span = modes // x
    row = lax.broadcasted_iota(jnp.int32, (modes, x), 0) // span
    col = lax.broadcasted_iota(jnp.int32, (modes, x), 1)
    pick = jnp.where(row == col, 1.0, 0.0).astype(bf16)
    row = lax.broadcasted_iota(jnp.int32, (x, modes), 0)
    col = lax.broadcasted_iota(jnp.int32, (x, modes), 1) // span
    pick_t = jnp.where(row == col, 1.0, 0.0).astype(bf16)
    row = lax.broadcasted_iota(jnp.int32, (modes, modes), 0)
    col = lax.broadcasted_iota(jnp.int32, (modes, modes), 1)
    same = row % span == col % span
    mm = partial(jnp.dot, preferred_element_type=f32)
    for source, (h_ref, l_ref) in ((bx_ref[...].T, (fh_ref, fl_ref)), (bx_ref[...], (bh_ref, bl_ref))):
        for part, ref in zip(split(source), (h_ref, l_ref)):
            wide = mm(mm(pick, part).astype(bf16), pick_t)
            ref[...] = jnp.where(same, wide, 0.0).astype(bf16)


def spread(basis_x, span):
    modes = basis_x.shape[0] * span
    return pl.pallas_call(
        spread_body,
        in_specs=[pl.BlockSpec(memory_space=pltpu.VMEM)],
        out_specs=[pl.BlockSpec(memory_space=pltpu.VMEM)] * 4,
        out_shape=[jax.ShapeDtypeStruct((modes, modes), bf16)] * 4,
        compiler_params=params(),
        cost_estimate=cost(8 * modes * modes * 64, 8 * modes * modes),
        name="spread",
    )(basis_x)


def local(right_side, basis_x, basis_y, basis_z, eig_x, eig_y, eig_z, steps):
    rows = right_side.shape[0]
    members, count = lax.axis_size("gx"), lax.axis_size("ta")
    member, place = lax.axis_index("gx"), lax.axis_index("ta")
    span = basis_y.shape[0] // members
    total = steps.shape[0]

    lengths = steps / total
    padded = jnp.concatenate([lengths, jnp.zeros((1,), f32)])
    lens = lax.dynamic_slice_in_dim(padded, place * rows, rows + 1)
    close = jnp.where(place * rows + jnp.arange(rows) == total - 1, 0.5, 0.0).astype(f32)
    part_y = lax.dynamic_slice_in_dim(eig_y, member * span, span)
    eigen = (eig_x[:, None, None] + part_y[None, :, None] + eig_z[None, None, :]).reshape(
        -1, eig_z.shape[0]
    )
    share = eigen.shape[0] // count
    eigen_own = lax.dynamic_slice_in_dim(eigen, place * share, share)

    volume = forward_yz(right_side, basis_y.T, basis_z, members)
    weights = spread(basis_x, span)
    terms = reduced_terms(padded, eigen_own, count, rows)
    volume = lax.all_to_all(volume, "gx", 0, 0, tiled=True)
    g, ends = eliminate(volume, eigen, weights[:2], lens, close, count)
    ends = lax.all_to_all(ends, "ta", 0, 0, tiled=True)
    ends = interface_solve(ends, terms)
    ends = lax.all_to_all(ends, "ta", 0, 0, tiled=True)
    cell = substitute(g, ends, eigen, weights[2:], lens, close, members)
    cell = lax.all_to_all(cell, "gx", 0, 0, tiled=True)
    return backward_yz(cell, basis_y, basis_z.T)


def solution(mesh):
    return jax.shard_map(
        local,
        mesh=mesh,
        in_specs=(P("ta", "gx", None, None), P(), P(), P(), P(), P(), P(), P()),
        out_specs=P("ta", "gx", None, None),
        check_vma=False,
    )
```

```python
from functools import partial

import jax
import jax.numpy as jnp
from jax import lax
from jax.experimental import pallas as pl
from jax.experimental.pallas import tpu as pltpu
from jax.sharding import PartitionSpec as P

f32, bf16 = jnp.float32, jnp.bfloat16
params = partial(pltpu.CompilerParams, vmem_limit_bytes=24 * 2**20)
VMEM = pl.BlockSpec(memory_space=pltpu.VMEM)
SMEM = pl.BlockSpec(memory_space=pltpu.SMEM)

PEERS = ((0, 0), (2, 0), (2, 1), (1, 0), (3, 0), (1, 1), (3, 1), (0, 1))


def peer(member, members, k, sign):
    chips, core = PEERS[k]
    ring = members // 2
    far = lax.rem(member // 2 + (sign * chips) % ring, ring)
    own = lax.rem(member, 2)
    return far * 2 + (1 - own if core else own)


def exchange(pieces):
    members = len(pieces)
    moved = [pieces[0]]
    for k in range(1, members):
        chips, core = PEERS[k]
        pairs = [(i, ((i // 2 + chips) * 2 + (i % 2 + core) % 2) % members) for i in range(members)]
        moved.append(lax.ppermute(pieces[k], "gx", pairs))
    return moved


def split(x):
    high = x.astype(bf16)
    return high, (x - high.astype(f32)).astype(bf16)


def left3(x):
    high, low = split(x)
    return jnp.concatenate([high, high, low], axis=1)


def right3(x):
    high, low = split(x)
    return jnp.concatenate([high, low, high], axis=0)


mm = partial(jnp.dot, preferred_element_type=f32)


def cost(flops, bytes_accessed):
    return pl.CostEstimate(flops=int(flops), bytes_accessed=int(bytes_accessed), transcendentals=0)


def whole(*shape):
    return pl.BlockSpec(shape, lambda k: (0,) * len(shape))


def array(*shape):
    return jax.ShapeDtypeStruct(shape, f32)


def gather_rows(source_ref, target_ref, sign):
    members = len(PEERS)
    span = target_ref.shape[0] // members
    member = lax.axis_index("gx")
    for k in range(members):
        start = pl.multiple_of(peer(member, members, k, sign) * span, span)
        target_ref[k * span : (k + 1) * span] = source_ref[pl.ds(start, span), :]


def forward_body(x_ref, by_ref, bz_ref, *refs):
    outs, (turn_ref, rows_ref, by3_ref, bz3_ref) = refs[:-4], refs[-4:]
    times, rows, y, z = x_ref.shape
    span = y // len(outs)

    @pl.when(pl.program_id(0) == 0)
    def _():
        turn_ref[...] = by_ref[...].T
        gather_rows(turn_ref, rows_ref, 1)
        by3_ref[...] = left3(rows_ref[...])
        bz3_ref[...] = right3(bz_ref[...])

    vol = [mm(left3(x_ref[t].reshape(rows * y, z)), bz3_ref[...]) for t in range(times)]
    for a in range(rows):
        plane = jnp.concatenate([v[a * y : (a + 1) * y] for v in vol], axis=1)
        plane = mm(by3_ref[...], right3(plane))
        for k, out in enumerate(outs):
            for t in range(times):
                out[t, pl.ds(a, span, stride=rows), :] = plane[
                    k * span : (k + 1) * span, t * z : (t + 1) * z
                ]


def forward_yz(x, by, bz, first, steps):
    _, a, y, z = x.shape
    members = len(PEERS)
    rows = a * y // members
    return pl.pallas_call(
        forward_body,
        grid=(steps // 2,),
        in_specs=[
            pl.BlockSpec((2, a, y, z), lambda k: (k + first // 2, 0, 0, 0)),
            whole(y, y),
            whole(z, z),
        ],
        out_specs=[pl.BlockSpec((2, rows, z), lambda k: (k, 0, 0))] * members,
        out_shape=[array(steps, rows, z)] * members,
        scratch_shapes=[
            pltpu.VMEM((y, y), f32),
            pltpu.VMEM((y, y), f32),
            pltpu.VMEM((y, 3 * y), bf16),
            pltpu.VMEM((3 * z, z), bf16),
        ],
        compiler_params=params(),
        cost_estimate=cost(6 * steps * a * y * z * (y + z), 8 * steps * a * y * z),
        name="forward_yz",
    )(x, by, bz)


def backward_body(by_ref, bz_ref, *refs):
    pieces, (out_ref, turn_ref, rows_ref, by3_ref, bz3_ref) = refs[: len(PEERS)], refs[-5:]
    times, rows, y, z = out_ref.shape
    span = y // len(pieces)

    @pl.when(pl.program_id(0) == 0)
    def _():
        turn_ref[...] = by_ref[...].T
        gather_rows(turn_ref, rows_ref, -1)
        by3_ref[...] = left3(rows_ref[...].T)
        bz3_ref[...] = right3(bz_ref[...].T)

    vol = [[] for t in range(times)]
    for a in range(rows):
        plane = jnp.concatenate(
            [
                jnp.concatenate(
                    [piece[t, pl.ds(a, span, stride=rows), :] for piece in pieces], axis=0
                )
                for t in range(times)
            ],
            axis=1,
        )
        plane = mm(by3_ref[...], right3(plane))
        for t in range(times):
            vol[t].append(plane[:, t * z : (t + 1) * z])
    for t in range(times):
        flat = jnp.concatenate(vol[t], axis=0)
        out_ref[t] = mm(left3(flat), bz3_ref[...]).reshape(rows, y, z)


def backward_yz(pieces, by, bz, first, total, earlier):
    members = len(pieces)
    y, z = by.shape[0], bz.shape[0]
    steps, rows = pieces[0].shape[:2]
    a = rows * members // y
    more = [] if earlier is None else [earlier]
    return pl.pallas_call(
        backward_body,
        grid=(steps // 2,),
        in_specs=[whole(y, y), whole(z, z)]
        + [pl.BlockSpec((2, rows, z), lambda k: (k, 0, 0))] * members
        + [pl.BlockSpec(memory_space=pl.ANY)] * len(more),
        out_specs=pl.BlockSpec((2, a, y, z), lambda k: (k + first // 2, 0, 0, 0)),
        out_shape=array(total, a, y, z),
        input_output_aliases={2 + members: 0} if more else {},
        scratch_shapes=[
            pltpu.VMEM((y, y), f32),
            pltpu.VMEM((y, y), f32),
            pltpu.VMEM((y, 3 * y), bf16),
            pltpu.VMEM((3 * z, z), bf16),
        ],
        compiler_params=params(),
        cost_estimate=cost(6 * steps * a * y * z * (y + z), 8 * steps * a * y * z),
        name="backward_yz",
    )(by, bz, *pieces, *more)


def length(steps_ref, at):
    total = steps_ref.shape[0]
    here = steps_ref[jnp.minimum(at, total - 1)] / total
    return jnp.where(at < total, here, 0.0)


def row_terms(eigen, steps_ref, at):
    now, then = length(steps_ref, at), length(steps_ref, at + 1)
    closing = jnp.where(at == steps_ref.shape[0] - 1, 0.5, 0.0)
    main = eigen * ((now + then) / 3.0) + closing
    sub = eigen * (now / 6.0) - 0.5
    sup = eigen * (then / 6.0) + 0.5
    return main, sub, sup


def mode_sums(ex_ref, ey_ref, ez_ref, j):
    x, z = ex_ref.shape[1], ez_ref.shape[1]
    along_x = jnp.broadcast_to(ex_ref[...], (z, x)).T
    return (along_x + ey_ref[j]) + ez_ref[...]


def fill_sums(ex_ref, ey_ref, ez_ref, sums_ref):
    x, members = ex_ref.shape[1], len(PEERS)
    span = ey_ref.shape[0] // members
    member = lax.axis_index("gx")
    for j in range(span):
        sums_ref[j * x : (j + 1) * x] = mode_sums(ex_ref, ey_ref, ez_ref, member * span + j)


def reduced_body(rows, steps_ref, ex_ref, ey_ref, ez_ref, cl_ref, e_ref, a_ref, k_ref, b_ref, q_ref, sums_ref):
    count, share = cl_ref.shape[:2]
    x, span = ex_ref.shape[1], ey_ref.shape[0] // len(PEERS)
    first = lax.axis_index("ta") * share
    sums_ref[...] = mode_sums(ex_ref, ey_ref, ez_ref, lax.axis_index("gx") * span + first // x)
    eigen = sums_ref[pl.ds(pl.multiple_of(lax.rem(first, x), share), share), :]

    def block(j, carry):
        inverses, subs, ratios = [], [], []
        for k in range(rows):
            main, sub, sup = row_terms(eigen, steps_ref, j * rows + k)
            inverse = 1.0 / (main - sub * ratios[-1] if k else main)
            inverses.append(inverse)
            subs.append(sub)
            ratios.append(sup * inverse)
        front = subs[0] * inverses[0]
        fronts = [front]
        for k in range(1, rows):
            front = -(subs[k] * inverses[k]) * front
            fronts.append(front)
        last = ratios[rows - 1]
        low = fronts[rows - 1]
        cl_ref[j] = low
        e_ref[j] = last
        for k in reversed(range(rows - 1)):
            low = fronts[k] - ratios[k] * low
            last = -ratios[k] * last
        a_ref[j] = low
        b_ref[j] = last
        return carry

    lax.fori_loop(0, count, block, 0, unroll=4)

    def sweep(j, q_before):
        v_last, w_last, v_first, w_first = cl_ref[j], e_ref[j], a_ref[j], b_ref[j]
        scale = 1.0 / (1.0 - v_first * q_before)
        back = w_first * scale
        q_now = w_last + v_last * q_before * back
        e_now = v_last * scale
        cl_ref[j] = e_now * q_before
        e_ref[j] = e_now
        a_ref[j] = scale
        k_ref[j] = v_first * scale
        b_ref[j] = back
        q_ref[j] = q_now
        return q_now

    lax.fori_loop(0, count, sweep, jnp.zeros_like(eigen))


def reduced_terms(steps, sums, count, rows, share):
    x, z = sums[0].shape[1], sums[2].shape[1]
    return pl.pallas_call(
        partial(reduced_body, rows),
        in_specs=[SMEM, VMEM, SMEM, VMEM],
        out_specs=[VMEM] * 6,
        out_shape=[array(count, share, z)] * 6,
        scratch_shapes=[pltpu.VMEM((x, z), f32)],
        compiler_params=params(),
        cost_estimate=cost(40 * rows * count * share * z, 24 * count * share * z),
        name="reduced_terms",
    )(steps, *sums)


def interface_body(g_ref, cl_ref, e_ref, a_ref, k_ref, b_ref, q_ref, out_ref, fh_ref):
    count = g_ref.shape[0]
    zero = jnp.zeros(g_ref.shape[2:], f32)

    def down(j, before):
        first, last = g_ref[j, 0], g_ref[j, 1]
        out_ref[j, 0] = before
        fh_ref[j] = a_ref[j] * first - k_ref[j] * before
        return (last + cl_ref[j] * first) - e_ref[j] * before

    lax.fori_loop(0, count, down, zero, unroll=8)

    def up(i, after):
        j = count - 1 - i
        out_ref[j, 1] = after

        @pl.when(j < count - 1)
        def _():
            out_ref[j + 1, 0] = out_ref[j + 1, 0] - q_ref[j] * after

        return fh_ref[j] - b_ref[j] * after

    lax.fori_loop(0, count, up, zero, unroll=8)


def interface_solve(g, terms):
    return pl.pallas_call(
        interface_body,
        in_specs=[VMEM] * 7,
        out_specs=VMEM,
        out_shape=array(*g.shape),
        scratch_shapes=[pltpu.VMEM(g.shape[:1] + g.shape[2:], f32)],
        compiler_params=params(),
        cost_estimate=cost(6 * g.size, 20 * g.size),
        name="interface_solve",
    )(g, *terms)


def eliminate_body(first, total, steps_ref, ex_ref, ey_ref, ez_ref, bx_ref, *refs):
    pieces, refs = refs[: len(PEERS)], refs[len(PEERS) :]
    earlier, refs = (refs[:2], refs[2:]) if first else ((), refs)
    closes = first + pl.num_programs(0) == total
    g_ref, ratio_ref, refs = refs[0], refs[1], refs[2:]
    ends_ref, refs = (refs[0], refs[1:]) if len(refs) == 4 else (None, refs)
    sums_ref, rows_ref, bx3_ref = refs
    step = pl.program_id(0)
    modes, lanes = g_ref.shape[1:]
    x = bx_ref.shape[0]
    span = x // len(pieces)
    t = step + first

    @pl.when(step == 0)
    def _():
        gather_rows(bx_ref, rows_ref, -1)
        bx3_ref[...] = left3(rows_ref[...].T)
        fill_sums(ex_ref, ey_ref, ez_ref, sums_ref)
        if first:
            g_ref[:first] = earlier[0][...]
            ratio_ref[:first] = earlier[1][...]

    spectral = []
    for j in range(0, modes // x, 2):
        plane = jnp.concatenate(
            [
                jnp.concatenate([piece[0, i * span : (i + 1) * span, :] for piece in pieces], axis=0)
                for i in (j, j + 1)
            ],
            axis=1,
        )
        plane = mm(bx3_ref[...], right3(plane))
        spectral += [plane[:, :lanes], plane[:, lanes:]]
    spectral = jnp.concatenate(spectral, axis=0)
    main, sub, sup = row_terms(sums_ref[...], steps_ref, lax.axis_index("ta") * total + t)

    def begin():
        inverse = 1.0 / main
        ratio_ref[t] = sup * inverse
        g_ref[t] = spectral * inverse

    def follow():
        inverse = 1.0 / (main - sub * ratio_ref[t - 1])
        ratio_ref[t] = sup * inverse
        g_ref[t] = (spectral - sub * g_ref[t - 1]) * inverse

    if first:
        follow()
    else:
        pl.when(step == 0)(begin)
        pl.when(step > 0)(follow)

    if ends_ref is not None:

        @pl.when(t == total - 1)
        def _():
            split_shape = (ends_ref.shape[0], modes // ends_ref.shape[0], lanes)
            now = g_ref[total - 1]
            ends_ref[:, 1] = now.reshape(split_shape)
            for k in reversed(range(total - 1)):
                now = g_ref[k] - ratio_ref[k] * now
                g_ref[k] = now
            ends_ref[:, 0] = now.reshape(split_shape)


def eliminate(pieces, sums, bx, steps, count, first, total, earlier):
    n, rows, z = pieces[0].shape
    x = bx.shape[0]
    modes = rows * len(pieces)
    last = first + n == total
    out = array(first + n, modes, z)
    outs = [out] + ([array(count, 2, modes // count, z)] if last else [out])
    scratch = [
        pltpu.VMEM((modes, z), f32),
        pltpu.VMEM((x, x), f32),
        pltpu.VMEM((x, 3 * x), bf16),
    ]

    def kernel(*refs):
        if last:
            at = len(refs) - 4
            refs = refs[: at - 1] + (refs[at], refs[at - 1]) + refs[at + 1 :]
        eliminate_body(first, total, *refs)

    return pl.pallas_call(
        kernel,
        grid=(n,),
        in_specs=[SMEM, whole(1, x), SMEM, whole(1, z), whole(x, x)]
        + [pl.BlockSpec((1, rows, z), lambda k: (k, 0, 0))] * len(pieces)
        + [whole(*e.shape) for e in earlier],
        out_specs=[whole(*o.shape) for o in outs],
        out_shape=outs,
        scratch_shapes=([pltpu.VMEM(out.shape, f32)] if last else []) + scratch,
        compiler_params=params(),
        cost_estimate=cost(6 * n * modes * x * z, 8 * n * modes * z),
        name="eliminate",
    )(steps, *sums, bx, *pieces, *earlier)


def return_body(first, total, steps_ref, ex_ref, ey_ref, ez_ref, bx_ref, *refs):
    members = len(PEERS)
    given, refs = (refs[:1], refs[1:]) if first else (refs[:2], refs[2:])
    outs, refs = refs[:members], refs[members:]
    sol_ref, refs = (given[0], refs) if first else (refs[0], refs[1:])
    step = pl.program_id(0)
    x, lanes = bx_ref.shape[0], ez_ref.shape[1]
    span = x // members
    rows_ref, bx3_ref = refs[-2:]

    @pl.when(step == 0)
    def _():
        gather_rows(bx_ref, rows_ref, 1)
        bx3_ref[...] = left3(rows_ref[...])

    if not first:
        g_ref, ends_ref = given
        sums_ref = refs[0]
        modes = g_ref.shape[1]

        @pl.when(step == 0)
        def _():
            fill_sums(ex_ref, ey_ref, ez_ref, sums_ref)
            eigen = sums_ref[...]
            begin = lax.axis_index("ta") * total
            before = ends_ref[:, 0].reshape(modes, lanes)
            after = ends_ref[:, 1].reshape(modes, lanes)
            ratios, values = [], []
            for k in range(total):
                main, sub, sup = row_terms(eigen, steps_ref, begin + k)
                inverse = 1.0 / (main - sub * ratios[-1] if k else main)
                ratios.append(sup * inverse)
                value = -(sub * inverse) * (values[-1] if k else before)
                if k == total - 1:
                    value = value - ratios[-1] * after
                values.append(value)
            now = values[total - 1]
            sol_ref[total - 1] = g_ref[total - 1] + now
            for k in reversed(range(total - 1)):
                now = values[k] - ratios[k] * now
                sol_ref[k] = g_ref[k] + now

    for j in range(0, sol_ref.shape[1] // x, 2):
        plane = jnp.concatenate(
            [sol_ref[step + first, i * x : (i + 1) * x, :] for i in (j, j + 1)], axis=1
        )
        plane = mm(bx3_ref[...], right3(plane))
        for k, out in enumerate(outs):
            for i in (0, 1):
                out[0, (j + i) * span : (j + i + 1) * span, :] = plane[
                    k * span : (k + 1) * span, i * lanes : (i + 1) * lanes
                ]


def return_x(given, sums, bx, steps, first, n):
    total, modes, z = given[0].shape
    x, members = bx.shape[0], len(PEERS)
    rows = modes // members
    whole_sol = n == total
    outs = [array(n, rows, z)] * members
    out_specs = [pl.BlockSpec((1, rows, z), lambda k: (k, 0, 0))] * members
    scratch = [pltpu.VMEM((x, x), f32), pltpu.VMEM((x, 3 * x), bf16)]
    if not first:
        scratch = [pltpu.VMEM((modes, z), f32)] + scratch
        if whole_sol:
            scratch = [pltpu.VMEM((total, modes, z), f32)] + scratch
        else:
            outs, out_specs = outs + [array(total, modes, z)], out_specs + [whole(total, modes, z)]
    return pl.pallas_call(
        partial(return_body, first, total),
        grid=(n,),
        in_specs=[SMEM, whole(1, x), SMEM, whole(1, z), whole(x, x)]
        + [whole(*g.shape) for g in given],
        out_specs=out_specs,
        out_shape=outs,
        scratch_shapes=scratch,
        compiler_params=params(),
        cost_estimate=cost(6 * n * modes * x * z, 8 * n * modes * z),
        name="return_x",
    )(steps, *sums, bx, *given)


CHUNKS = 1


def local(right_side, basis_x, basis_y, basis_z, eig_x, eig_y, eig_z, steps):
    rows = right_side.shape[0]
    count = lax.axis_size("ta")
    sums = (eig_x[None, :], eig_y, eig_z[None, :])
    n = rows // CHUNKS
    share = basis_x.shape[0] * basis_y.shape[0] // (lax.axis_size("gx") * count)
    right_side = pltpu.with_memory_space_constraint(right_side, pltpu.HBM)

    sent = [forward_yz(right_side, basis_y, basis_z, first, n) for first in range(0, rows, n)]
    state = ()
    for c, pieces in enumerate(sent):
        state = eliminate(exchange(pieces), sums, basis_x, steps, count, c * n, rows, state)
    g, ends = state
    terms = reduced_terms(steps, sums, count, rows, share)
    ends = lax.all_to_all(ends, "ta", 0, 0, tiled=True)
    ends = interface_solve(ends, terms)
    ends = lax.all_to_all(ends, "ta", 0, 0, tiled=True)
    given, sent = (g, ends), []
    for c in range(CHUNKS):
        pieces = return_x(given, sums, basis_x, steps, c * n, n)
        given = given if c else pieces[len(PEERS) :]
        sent.append(pieces[: len(PEERS)])
    result = None
    for c, pieces in enumerate(sent):
        result = backward_yz(exchange(pieces), basis_y, basis_z, c * n, rows, result)
    return result


def solution(mesh):
    return jax.shard_map(
        local,
        mesh=mesh,
        in_specs=(P("ta", "gx", None, None), P(), P(), P(), P(), P(), P(), P()),
        out_specs=P("ta", "gx", None, None),
        check_vma=False,
    )
```

```python
from functools import partial

import jax
import jax.numpy as jnp
from jax import lax
from jax.experimental import pallas as pl
from jax.experimental.pallas import tpu as pltpu
from jax.sharding import PartitionSpec as P

f32, bf16 = jnp.float32, jnp.bfloat16
params = partial(pltpu.CompilerParams, vmem_limit_bytes=24 * 2**20)
VMEM = pl.BlockSpec(memory_space=pltpu.VMEM)
SMEM = pl.BlockSpec(memory_space=pltpu.SMEM)

PEERS = ((0, 0), (2, 0), (2, 1), (1, 0), (3, 0), (1, 1), (3, 1), (0, 1))


def peer(member, members, place, sign):
    chips, core = place
    ring = members // 2
    far = lax.rem(member // 2 + (sign * chips) % ring, ring)
    own = lax.rem(member, 2)
    return far * 2 + (1 - own if core else own)


def exchange(pieces, peers):
    members = len(pieces)
    moved = [pieces[0]]
    for k in range(1, members):
        chips, core = peers[k]
        pairs = [(i, ((i // 2 + chips) * 2 + (i % 2 + core) % 2) % members) for i in range(members)]
        moved.append(lax.ppermute(pieces[k], "gx", pairs))
    return moved


def split(x):
    high = x.astype(bf16)
    return high, (x - high.astype(f32)).astype(bf16)


def left3(x):
    high, low = split(x)
    return jnp.concatenate([high, high, low], axis=1)


def right3(x):
    high, low = split(x)
    return jnp.concatenate([high, low, high], axis=0)


mm = partial(jnp.dot, preferred_element_type=f32)


def cost(flops, bytes_accessed):
    return pl.CostEstimate(flops=int(flops), bytes_accessed=int(bytes_accessed), transcendentals=0)


def whole(*shape):
    return pl.BlockSpec(shape, lambda k: (0,) * len(shape))


def array(*shape):
    return jax.ShapeDtypeStruct(shape, f32)


def gather_rows(source_ref, target_ref, peers, sign):
    members = len(peers)
    span = target_ref.shape[0] // members
    member = lax.axis_index("gx")
    for k, place in enumerate(peers):
        start = pl.multiple_of(peer(member, members, place, sign) * span, span)
        target_ref[k * span : (k + 1) * span] = source_ref[pl.ds(start, span), :]


def forward_body(x_ref, by_ref, bz_ref, *refs):
    outs, (turn_ref, rows_ref, by3_ref, bz3_ref) = refs[:-4], refs[-4:]
    times, rows, y, z = x_ref.shape
    span = y // len(outs)

    @pl.when(pl.program_id(0) == 0)
    def _():
        turn_ref[...] = by_ref[...].T
        gather_rows(turn_ref, rows_ref, PEERS, 1)
        by3_ref[...] = left3(rows_ref[...])
        bz3_ref[...] = right3(bz_ref[...])

    vol = [mm(left3(x_ref[t].reshape(rows * y, z)), bz3_ref[...]) for t in range(times)]
    for a in range(rows):
        plane = jnp.concatenate([v[a * y : (a + 1) * y] for v in vol], axis=1)
        plane = mm(by3_ref[...], right3(plane))
        for k, out in enumerate(outs):
            for t in range(times):
                out[t, pl.ds(a, span, stride=rows), :] = plane[
                    k * span : (k + 1) * span, t * z : (t + 1) * z
                ]


def forward_yz(x, by, bz):
    t, a, y, z = x.shape
    members = len(PEERS)
    rows = a * y // members
    return pl.pallas_call(
        forward_body,
        grid=(t // 2,),
        in_specs=[
            pl.BlockSpec((2, a, y, z), lambda k: (k, 0, 0, 0)),
            whole(y, y),
            whole(z, z),
        ],
        out_specs=[pl.BlockSpec((2, rows, z), lambda k: (k, 0, 0))] * members,
        out_shape=[array(t, rows, z)] * members,
        scratch_shapes=[
            pltpu.VMEM((y, y), f32),
            pltpu.VMEM((y, y), f32),
            pltpu.VMEM((y, 3 * y), bf16),
            pltpu.VMEM((3 * z, z), bf16),
        ],
        compiler_params=params(),
        cost_estimate=cost(6 * t * a * y * z * (y + z), 8 * t * a * y * z),
        name="forward_yz",
    )(x, by, bz)


def backward_body(by_ref, bz_ref, *refs):
    pieces, (out_ref, turn_ref, rows_ref, by3_ref, bz3_ref) = refs[:-5], refs[-5:]
    times, rows, y, z = out_ref.shape
    span = y // len(pieces)

    @pl.when(pl.program_id(0) == 0)
    def _():
        turn_ref[...] = by_ref[...].T
        gather_rows(turn_ref, rows_ref, PEERS, -1)
        by3_ref[...] = left3(rows_ref[...].T)
        bz3_ref[...] = right3(bz_ref[...].T)

    vol = [[] for t in range(times)]
    for a in range(rows):
        plane = jnp.concatenate(
            [
                jnp.concatenate(
                    [piece[t, pl.ds(a, span, stride=rows), :] for piece in pieces], axis=0
                )
                for t in range(times)
            ],
            axis=1,
        )
        plane = mm(by3_ref[...], right3(plane))
        for t in range(times):
            vol[t].append(plane[:, t * z : (t + 1) * z])
    for t in range(times):
        flat = jnp.concatenate(vol[t], axis=0)
        out_ref[t] = mm(left3(flat), bz3_ref[...]).reshape(rows, y, z)


def backward_yz(pieces, by, bz):
    members = len(pieces)
    y, z = by.shape[0], bz.shape[0]
    t, rows = pieces[0].shape[:2]
    a = rows * members // y
    return pl.pallas_call(
        backward_body,
        grid=(t // 2,),
        in_specs=[whole(y, y), whole(z, z)]
        + [pl.BlockSpec((2, rows, z), lambda k: (k, 0, 0))] * members,
        out_specs=pl.BlockSpec((2, a, y, z), lambda k: (k, 0, 0, 0)),
        out_shape=array(t, a, y, z),
        scratch_shapes=[
            pltpu.VMEM((y, y), f32),
            pltpu.VMEM((y, y), f32),
            pltpu.VMEM((y, 3 * y), bf16),
            pltpu.VMEM((3 * z, z), bf16),
        ],
        compiler_params=params(),
        cost_estimate=cost(6 * t * a * y * z * (y + z), 8 * t * a * y * z),
        name="backward_yz",
    )(by, bz, *pieces)


def length(steps_ref, at):
    total = steps_ref.shape[0]
    here = steps_ref[jnp.minimum(at, total - 1)] / total
    return jnp.where(at < total, here, 0.0)


def row_terms(eigen, steps_ref, at):
    now, then = length(steps_ref, at), length(steps_ref, at + 1)
    closing = jnp.where(at == steps_ref.shape[0] - 1, 0.5, 0.0)
    main = eigen * ((now + then) / 3.0) + closing
    sub = eigen * (now / 6.0) - 0.5
    sup = eigen * (then / 6.0) + 0.5
    return main, sub, sup


def mode_sums(ex_ref, ey_ref, ez_ref, j):
    x, z = ex_ref.shape[1], ez_ref.shape[1]
    along_x = jnp.broadcast_to(ex_ref[...], (z, x)).T
    return (along_x + ey_ref[j]) + ez_ref[...]


def fill_sums(ex_ref, ey_ref, ez_ref, sums_ref):
    x, members = ex_ref.shape[1], len(PEERS)
    span = ey_ref.shape[0] // members
    member = lax.axis_index("gx")
    for j in range(span):
        sums_ref[j * x : (j + 1) * x] = mode_sums(ex_ref, ey_ref, ez_ref, member * span + j)


def reduced_body(rows, steps_ref, ex_ref, ey_ref, ez_ref, cl_ref, e_ref, a_ref, k_ref, b_ref, q_ref, sums_ref):
    count, share = cl_ref.shape[:2]
    x, span = ex_ref.shape[1], ey_ref.shape[0] // len(PEERS)
    first = lax.axis_index("ta") * share
    sums_ref[...] = mode_sums(ex_ref, ey_ref, ez_ref, lax.axis_index("gx") * span + first // x)
    eigen = sums_ref[pl.ds(pl.multiple_of(lax.rem(first, x), share), share), :]

    def block(j, carry):
        inverses, subs, ratios = [], [], []
        for k in range(rows):
            main, sub, sup = row_terms(eigen, steps_ref, j * rows + k)
            inverse = 1.0 / (main - sub * ratios[-1] if k else main)
            inverses.append(inverse)
            subs.append(sub)
            ratios.append(sup * inverse)
        front = subs[0] * inverses[0]
        fronts = [front]
        for k in range(1, rows):
            front = -(subs[k] * inverses[k]) * front
            fronts.append(front)
        last = ratios[rows - 1]
        low = fronts[rows - 1]
        cl_ref[j] = low
        e_ref[j] = last
        for k in reversed(range(rows - 1)):
            low = fronts[k] - ratios[k] * low
            last = -ratios[k] * last
        a_ref[j] = low
        b_ref[j] = last
        return carry

    lax.fori_loop(0, count, block, 0, unroll=4)

    def sweep(j, q_before):
        v_last, w_last, v_first, w_first = cl_ref[j], e_ref[j], a_ref[j], b_ref[j]
        scale = 1.0 / (1.0 - v_first * q_before)
        back = w_first * scale
        q_now = w_last + v_last * q_before * back
        e_now = v_last * scale
        cl_ref[j] = e_now * q_before
        e_ref[j] = e_now
        a_ref[j] = scale
        k_ref[j] = v_first * scale
        b_ref[j] = back
        q_ref[j] = q_now
        return q_now

    lax.fori_loop(0, count, sweep, jnp.zeros_like(eigen))


def reduced_terms(steps, sums, count, rows, share):
    x, z = sums[0].shape[1], sums[2].shape[1]
    return pl.pallas_call(
        partial(reduced_body, rows),
        in_specs=[SMEM, VMEM, SMEM, VMEM],
        out_specs=[VMEM] * 6,
        out_shape=[array(count, share, z)] * 6,
        scratch_shapes=[pltpu.VMEM((x, z), f32)],
        compiler_params=params(),
        cost_estimate=cost(40 * rows * count * share * z, 24 * count * share * z),
        name="reduced_terms",
    )(steps, *sums)


def interface_body(g_ref, cl_ref, e_ref, a_ref, k_ref, b_ref, q_ref, out_ref, fh_ref):
    count = g_ref.shape[0]
    zero = jnp.zeros(g_ref.shape[2:], f32)

    def down(j, before):
        first, last = g_ref[j, 0], g_ref[j, 1]
        out_ref[j, 0] = before
        fh_ref[j] = a_ref[j] * first - k_ref[j] * before
        return (last + cl_ref[j] * first) - e_ref[j] * before

    lax.fori_loop(0, count, down, zero, unroll=8)

    def up(i, after):
        j = count - 1 - i
        out_ref[j, 1] = after

        @pl.when(j < count - 1)
        def _():
            out_ref[j + 1, 0] = out_ref[j + 1, 0] - q_ref[j] * after

        return fh_ref[j] - b_ref[j] * after

    lax.fori_loop(0, count, up, zero, unroll=8)


def interface_solve(g, terms):
    return pl.pallas_call(
        interface_body,
        in_specs=[VMEM] * 7,
        out_specs=VMEM,
        out_shape=array(*g.shape),
        scratch_shapes=[pltpu.VMEM(g.shape[:1] + g.shape[2:], f32)],
        compiler_params=params(),
        cost_estimate=cost(6 * g.size, 20 * g.size),
        name="interface_solve",
    )(g, *terms)


def eliminate_body(steps_ref, ex_ref, ey_ref, ez_ref, bx_ref, *refs):
    pieces, (g_ref, ends_ref, ratio_ref, sums_ref, rows_ref, bx3_ref) = refs[:-6], refs[-6:]
    step = pl.program_id(0)
    total, modes, lanes = g_ref.shape
    times = pieces[0].shape[0]
    x = bx_ref.shape[0]
    span = x // len(pieces)

    @pl.when(step == 0)
    def _():
        gather_rows(bx_ref, rows_ref, PEERS, -1)
        bx3_ref[...] = left3(rows_ref[...].T)
        fill_sums(ex_ref, ey_ref, ez_ref, sums_ref)

    spectral = [[] for k in range(times)]
    for j in range(modes // x):
        plane = jnp.concatenate(
            [
                jnp.concatenate([piece[k, j * span : (j + 1) * span, :] for piece in pieces], axis=0)
                for k in range(times)
            ],
            axis=1,
        )
        plane = mm(bx3_ref[...], right3(plane))
        for k in range(times):
            spectral[k].append(plane[:, k * lanes : (k + 1) * lanes])
    for k in range(times):
        t = step * times + k
        values = jnp.concatenate(spectral[k], axis=0)
        main, sub, sup = row_terms(sums_ref[...], steps_ref, lax.axis_index("ta") * total + t)

        def begin():
            inverse = 1.0 / main
            ratio_ref[t] = sup * inverse
            g_ref[t] = values * inverse

        def follow():
            inverse = 1.0 / (main - sub * ratio_ref[t - 1])
            ratio_ref[t] = sup * inverse
            g_ref[t] = (values - sub * g_ref[t - 1]) * inverse

        if k:
            follow()
        else:
            pl.when(step == 0)(begin)
            pl.when(step > 0)(follow)

    @pl.when(step == pl.num_programs(0) - 1)
    def _():
        split_shape = (ends_ref.shape[0], modes // ends_ref.shape[0], lanes)
        now = g_ref[total - 1]
        ends_ref[:, 1] = now.reshape(split_shape)
        for k in reversed(range(total - 1)):
            now = g_ref[k] - ratio_ref[k] * now
            g_ref[k] = now
        ends_ref[:, 0] = now.reshape(split_shape)


def eliminate(pieces, sums, bx, steps, count):
    t, rows, z = pieces[0].shape
    x = bx.shape[0]
    modes = rows * len(pieces)
    outs = [array(t, modes, z), array(count, 2, modes // count, z)]
    return pl.pallas_call(
        eliminate_body,
        grid=(t // 2,),
        in_specs=[SMEM, whole(1, x), SMEM, whole(1, z), whole(x, x)]
        + [pl.BlockSpec((2, rows, z), lambda k: (k, 0, 0))] * len(pieces),
        out_specs=[whole(*o.shape) for o in outs],
        out_shape=outs,
        scratch_shapes=[
            pltpu.VMEM((t, modes, z), f32),
            pltpu.VMEM((modes, z), f32),
            pltpu.VMEM((x, x), f32),
            pltpu.VMEM((x, 3 * x), bf16),
        ],
        compiler_params=params(),
        cost_estimate=cost(6 * t * modes * x * z, 8 * t * modes * z),
        name="eliminate",
    )(steps, *sums, bx, *pieces)


def return_body(steps_ref, ex_ref, ey_ref, ez_ref, bx_ref, g_ref, ends_ref, *refs):
    outs, (sol_ref, sums_ref, rows_ref, bx3_ref) = refs[:-4], refs[-4:]
    step = pl.program_id(0)
    total, modes, lanes = g_ref.shape
    times = outs[0].shape[0]
    x = bx_ref.shape[0]
    span = x // len(outs)

    @pl.when(step == 0)
    def _():
        gather_rows(bx_ref, rows_ref, PEERS, 1)
        bx3_ref[...] = left3(rows_ref[...])
        fill_sums(ex_ref, ey_ref, ez_ref, sums_ref)
        eigen = sums_ref[...]
        begin = lax.axis_index("ta") * total
        before = ends_ref[:, 0].reshape(modes, lanes)
        after = ends_ref[:, 1].reshape(modes, lanes)
        ratios, values = [], []
        for k in range(total):
            main, sub, sup = row_terms(eigen, steps_ref, begin + k)
            inverse = 1.0 / (main - sub * ratios[-1] if k else main)
            ratios.append(sup * inverse)
            value = -(sub * inverse) * (values[-1] if k else before)
            if k == total - 1:
                value = value - ratios[-1] * after
            values.append(value)
        now = values[total - 1]
        sol_ref[total - 1] = g_ref[total - 1] + now
        for k in reversed(range(total - 1)):
            now = values[k] - ratios[k] * now
            sol_ref[k] = g_ref[k] + now

    for j in range(modes // x):
        plane = jnp.concatenate(
            [sol_ref[step * times + k, j * x : (j + 1) * x, :] for k in range(times)], axis=1
        )
        plane = mm(bx3_ref[...], right3(plane))
        for i, out in enumerate(outs):
            for k in range(times):
                out[k, j * span : (j + 1) * span, :] = plane[
                    i * span : (i + 1) * span, k * lanes : (k + 1) * lanes
                ]


def return_x(g, ends, sums, bx, steps):
    t, modes, z = g.shape
    x, members = bx.shape[0], len(PEERS)
    rows = modes // members
    return pl.pallas_call(
        return_body,
        grid=(t // 2,),
        in_specs=[SMEM, whole(1, x), SMEM, whole(1, z), whole(x, x), whole(*g.shape), whole(*ends.shape)],
        out_specs=[pl.BlockSpec((2, rows, z), lambda k: (k, 0, 0))] * members,
        out_shape=[array(t, rows, z)] * members,
        scratch_shapes=[
            pltpu.VMEM((t, modes, z), f32),
            pltpu.VMEM((modes, z), f32),
            pltpu.VMEM((x, x), f32),
            pltpu.VMEM((x, 3 * x), bf16),
        ],
        compiler_params=params(),
        cost_estimate=cost(6 * t * modes * x * z, 8 * t * modes * z),
        name="return_x",
    )(steps, *sums, bx, g, ends)


def local(right_side, basis_x, basis_y, basis_z, eig_x, eig_y, eig_z, steps):
    rows = right_side.shape[0]
    count = lax.axis_size("ta")
    sums = (eig_x[None, :], eig_y, eig_z[None, :])
    share = basis_x.shape[0] * basis_y.shape[0] // (lax.axis_size("gx") * count)
    hbm = lambda value: pltpu.with_memory_space_constraint(value, pltpu.HBM)

    sent = forward_yz(hbm(right_side), hbm(basis_y), hbm(basis_z))
    moved = exchange(sent, PEERS)
    terms = list(reduced_terms(steps, sums, count, rows, share))
    moved[0], terms[0] = lax.optimization_barrier((moved[0], terms[0]))
    g, ends = eliminate(moved, sums, basis_x, steps, count)
    ends = lax.all_to_all(ends, "ta", 0, 0, tiled=True)
    ends = interface_solve(ends, terms)
    ends = lax.all_to_all(ends, "ta", 0, 0, tiled=True)
    moved = exchange(return_x(g, ends, sums, basis_x, steps), PEERS)
    return backward_yz(moved, basis_y, basis_z)


def solution(mesh):
    return jax.shard_map(
        local,
        mesh=mesh,
        in_specs=(P("ta", "gx", None, None), P(), P(), P(), P(), P(), P(), P()),
        out_specs=P("ta", "gx", None, None),
        check_vma=False,
    )
```

```python
from functools import partial

import jax
import jax.numpy as jnp
from jax import lax
from jax.experimental import pallas as pl
from jax.experimental.pallas import tpu as pltpu
from jax.sharding import PartitionSpec as P

f32, bf16 = jnp.float32, jnp.bfloat16
params = partial(pltpu.CompilerParams, vmem_limit_bytes=12 * 2**20)
VMEM = pl.BlockSpec(memory_space=pltpu.VMEM)
SMEM = pl.BlockSpec(memory_space=pltpu.SMEM)
ANY = pl.BlockSpec(memory_space=pl.ANY)

PEERS = ((0, 0), (2, 0), (2, 1), (1, 0), (3, 0), (1, 1), (3, 1), (0, 1))


def peer(member, members, place, sign):
    chips, core = place
    ring = members // 2
    far = lax.rem(member // 2 + (sign * chips) % ring, ring)
    own = lax.rem(member, 2)
    return far * 2 + (1 - own if core else own)


def exchange(pieces, peers):
    members = len(pieces)
    moved = [pieces[0]]
    for k in range(1, members):
        chips, core = peers[k]
        pairs = [(i, ((i // 2 + chips) * 2 + (i % 2 + core) % 2) % members) for i in range(members)]
        moved.append(lax.ppermute(pieces[k], "gx", pairs))
    return moved


def split(x):
    high = x.astype(bf16)
    return high, (x - high.astype(f32)).astype(bf16)


def left3(x):
    high, low = split(x)
    return jnp.concatenate([high, high, low], axis=1)


def right3(x):
    high, low = split(x)
    return jnp.concatenate([high, low, high], axis=0)


mm = partial(jnp.dot, preferred_element_type=f32)


def cost(flops, bytes_accessed):
    return pl.CostEstimate(flops=int(flops), bytes_accessed=int(bytes_accessed), transcendentals=0)


def array(*shape):
    return jax.ShapeDtypeStruct(shape, f32)


def gather_rows(source_ref, target_ref, peers, sign):
    members = len(peers)
    span = target_ref.shape[0] // members
    member = lax.axis_index("gx")
    for k, place in enumerate(peers):
        start = pl.multiple_of(peer(member, members, place, sign) * span, span)
        target_ref[k * span : (k + 1) * span] = source_ref[pl.ds(start, span), :]


def forward_body(x_any, by_any, bz_any, *refs):
    outs, refs = refs[: len(PEERS)], refs[len(PEERS) :]
    x_ref, by_ref, bz_ref, turn_ref, rows_ref, by3_ref, bz3_ref, x_sem, b_sem = refs
    total, rows, y, z = x_ref.shape
    span = y // len(outs)
    tables = [
        pltpu.make_async_copy(source, target, b_sem.at[k])
        for k, (source, target) in enumerate(((by_any, by_ref), (bz_any, bz_ref)))
    ]
    planes = [pltpu.make_async_copy(x_any.at[t], x_ref.at[t], x_sem.at[t]) for t in range(total)]
    for copy in tables + planes:
        copy.start()
    for copy in tables:
        copy.wait()
    turn_ref[...] = by_ref[...].T
    gather_rows(turn_ref, rows_ref, PEERS, 1)
    by3_ref[...] = left3(rows_ref[...])
    bz3_ref[...] = right3(bz_ref[...])

    for first in range(0, total, 4):
        times = range(first, first + 4)
        for t in times:
            planes[t].wait()
        vol = [mm(left3(x_ref[t].reshape(rows * y, z)), bz3_ref[...]) for t in times]
        for a in range(rows):
            plane = jnp.concatenate([v[a * y : (a + 1) * y] for v in vol], axis=1)
            plane = mm(by3_ref[...], right3(plane))
            for k, out in enumerate(outs):
                for i, t in enumerate(times):
                    out[t, pl.ds(a, span, stride=rows), :] = plane[
                        k * span : (k + 1) * span, i * z : (i + 1) * z
                    ]


def forward_yz(x, by, bz):
    t, a, y, z = x.shape
    members = len(PEERS)
    rows = a * y // members
    return pl.pallas_call(
        forward_body,
        in_specs=[ANY] * 3,
        out_specs=[VMEM] * members,
        out_shape=[array(t, rows, z)] * members,
        scratch_shapes=[
            pltpu.VMEM(x.shape, f32),
            pltpu.VMEM((y, y), f32),
            pltpu.VMEM((z, z), f32),
            pltpu.VMEM((y, y), f32),
            pltpu.VMEM((y, y), f32),
            pltpu.VMEM((y, 3 * y), bf16),
            pltpu.VMEM((3 * z, z), bf16),
            pltpu.SemaphoreType.DMA((t,)),
            pltpu.SemaphoreType.DMA((2,)),
        ],
        compiler_params=params(),
        cost_estimate=cost(6 * t * a * y * z * (y + z), 8 * t * a * y * z),
        name="forward_yz",
    )(x, by, bz)


def backward_body(by_ref, bz_ref, *refs):
    pieces, refs = refs[: len(PEERS)], refs[len(PEERS) :]
    out_any, out_ref, turn_ref, rows_ref, by3_ref, bz3_ref, sem = refs
    total, rows, y, z = out_ref.shape
    span = y // len(pieces)
    turn_ref[...] = by_ref[...].T
    gather_rows(turn_ref, rows_ref, PEERS, -1)
    by3_ref[...] = left3(rows_ref[...].T)
    bz3_ref[...] = right3(bz_ref[...].T)

    copies = []
    for first in range(0, total, 4):
        times = range(first, first + 4)
        vol = []
        for a in range(rows):
            plane = jnp.concatenate(
                [
                    jnp.concatenate(
                        [piece[t, pl.ds(a, span, stride=rows), :] for piece in pieces], axis=0
                    )
                    for t in times
                ],
                axis=1,
            )
            vol.append(mm(by3_ref[...], right3(plane)))
        for i, t in enumerate(times):
            flat = jnp.concatenate([v[:, i * z : (i + 1) * z] for v in vol], axis=0)
            out_ref[t] = mm(left3(flat), bz3_ref[...]).reshape(rows, y, z)
        for t in times:
            copies.append(pltpu.make_async_copy(out_ref.at[t], out_any.at[t], sem.at[t]))
            copies[-1].start()
    for copy in copies:
        copy.wait()


def backward_yz(pieces, by, bz):
    members = len(pieces)
    y, z = by.shape[0], bz.shape[0]
    t, rows = pieces[0].shape[:2]
    a = rows * members // y
    return pl.pallas_call(
        backward_body,
        in_specs=[VMEM] * (2 + members),
        out_specs=ANY,
        out_shape=array(t, a, y, z),
        scratch_shapes=[
            pltpu.VMEM((t, a, y, z), f32),
            pltpu.VMEM((y, y), f32),
            pltpu.VMEM((y, y), f32),
            pltpu.VMEM((y, 3 * y), bf16),
            pltpu.VMEM((3 * z, z), bf16),
            pltpu.SemaphoreType.DMA((t,)),
        ],
        compiler_params=params(),
        cost_estimate=cost(6 * t * a * y * z * (y + z), 8 * t * a * y * z),
        name="backward_yz",
    )(by, bz, *pieces)


def length(steps_ref, at):
    total = steps_ref.shape[0]
    here = steps_ref[jnp.minimum(at, total - 1)] / total
    return jnp.where(at < total, here, 0.0)


def row_terms(eigen, steps_ref, at):
    now, then = length(steps_ref, at), length(steps_ref, at + 1)
    closing = jnp.where(at == steps_ref.shape[0] - 1, 0.5, 0.0)
    main = eigen * ((now + then) / 3.0) + closing
    sub = eigen * (now / 6.0) - 0.5
    sup = eigen * (then / 6.0) + 0.5
    return main, sub, sup


def mode_sums(ex_ref, ey_ref, ez_ref, j):
    x, z = ex_ref.shape[1], ez_ref.shape[1]
    along_x = jnp.broadcast_to(ex_ref[...], (z, x)).T
    return (along_x + ey_ref[j]) + ez_ref[...]


def fill_sums(ex_ref, ey_ref, ez_ref, sums_ref):
    x, members = ex_ref.shape[1], len(PEERS)
    span = ey_ref.shape[0] // members
    member = lax.axis_index("gx")
    for j in range(span):
        sums_ref[j * x : (j + 1) * x] = mode_sums(ex_ref, ey_ref, ez_ref, member * span + j)


def reduced_body(rows, steps_ref, ex_ref, ey_ref, ez_ref, cl_ref, e_ref, a_ref, k_ref, b_ref, q_ref, sums_ref):
    count, share = cl_ref.shape[:2]
    x, span = ex_ref.shape[1], ey_ref.shape[0] // len(PEERS)
    first = lax.axis_index("ta") * share
    sums_ref[...] = mode_sums(ex_ref, ey_ref, ez_ref, lax.axis_index("gx") * span + first // x)
    eigen = sums_ref[pl.ds(pl.multiple_of(lax.rem(first, x), share), share), :]

    def block(j, carry):
        inverses, subs, ratios = [], [], []
        for k in range(rows):
            main, sub, sup = row_terms(eigen, steps_ref, j * rows + k)
            inverse = 1.0 / (main - sub * ratios[-1] if k else main)
            inverses.append(inverse)
            subs.append(sub)
            ratios.append(sup * inverse)
        front = subs[0] * inverses[0]
        fronts = [front]
        for k in range(1, rows):
            front = -(subs[k] * inverses[k]) * front
            fronts.append(front)
        last = ratios[rows - 1]
        low = fronts[rows - 1]
        cl_ref[j] = low
        e_ref[j] = last
        for k in reversed(range(rows - 1)):
            low = fronts[k] - ratios[k] * low
            last = -ratios[k] * last
        a_ref[j] = low
        b_ref[j] = last
        return carry

    lax.fori_loop(0, count, block, 0, unroll=4)

    def sweep(j, q_before):
        v_last, w_last, v_first, w_first = cl_ref[j], e_ref[j], a_ref[j], b_ref[j]
        scale = 1.0 / (1.0 - v_first * q_before)
        back = w_first * scale
        q_now = w_last + v_last * q_before * back
        e_now = v_last * scale
        cl_ref[j] = e_now * q_before
        e_ref[j] = e_now
        a_ref[j] = scale
        k_ref[j] = v_first * scale
        b_ref[j] = back
        q_ref[j] = q_now
        return q_now

    lax.fori_loop(0, count, sweep, jnp.zeros_like(eigen))


def reduced_terms(steps, sums, count, rows, share):
    x, z = sums[0].shape[1], sums[2].shape[1]
    return pl.pallas_call(
        partial(reduced_body, rows),
        in_specs=[SMEM, VMEM, SMEM, VMEM],
        out_specs=[VMEM] * 6,
        out_shape=[array(count, share, z)] * 6,
        scratch_shapes=[pltpu.VMEM((x, z), f32)],
        compiler_params=params(),
        cost_estimate=cost(40 * rows * count * share * z, 24 * count * share * z),
        name="reduced_terms",
    )(steps, *sums)


def interface_body(g_ref, cl_ref, e_ref, a_ref, k_ref, b_ref, q_ref, out_ref, fh_ref):
    count = g_ref.shape[0]
    zero = jnp.zeros(g_ref.shape[2:], f32)

    def down(j, before):
        first, last = g_ref[j, 0], g_ref[j, 1]
        out_ref[j, 0] = before
        fh_ref[j] = a_ref[j] * first - k_ref[j] * before
        return (last + cl_ref[j] * first) - e_ref[j] * before

    lax.fori_loop(0, count, down, zero, unroll=8)

    def up(i, after):
        j = count - 1 - i
        out_ref[j, 1] = after

        @pl.when(j < count - 1)
        def _():
            out_ref[j + 1, 0] = out_ref[j + 1, 0] - q_ref[j] * after

        return fh_ref[j] - b_ref[j] * after

    lax.fori_loop(0, count, up, zero, unroll=8)


def interface_solve(g, terms):
    return pl.pallas_call(
        interface_body,
        in_specs=[VMEM] * 7,
        out_specs=VMEM,
        out_shape=array(*g.shape),
        scratch_shapes=[pltpu.VMEM(g.shape[:1] + g.shape[2:], f32)],
        compiler_params=params(),
        cost_estimate=cost(6 * g.size, 20 * g.size),
        name="interface_solve",
    )(g, *terms)


def transform_pair(table, planes):
    lanes = planes[0].shape[1]
    both = mm(table, right3(jnp.concatenate(planes, axis=1)))
    return both[:, :lanes], both[:, lanes:]


def eliminate_body(steps_ref, ex_ref, ey_ref, ez_ref, bx_ref, *refs):
    pieces, refs = refs[: len(PEERS)], refs[len(PEERS) :]
    g_ref, ends_ref, ratio_ref, sums_ref, rows_ref, bx3_ref = refs
    total, modes, lanes = g_ref.shape
    x = bx_ref.shape[0]
    span = x // len(pieces)
    gather_rows(bx_ref, rows_ref, PEERS, -1)
    bx3_ref[...] = left3(rows_ref[...].T)
    fill_sums(ex_ref, ey_ref, ez_ref, sums_ref)
    begin = lax.axis_index("ta") * total

    for t in range(0, total, 2):
        for j in range(modes // x):
            mine = slice(j * x, (j + 1) * x)
            spectral = transform_pair(
                bx3_ref[...],
                [
                    jnp.concatenate([piece[k, j * span : (j + 1) * span, :] for piece in pieces], axis=0)
                    for k in (t, t + 1)
                ],
            )
            for k, values in zip((t, t + 1), spectral):
                main, sub, sup = row_terms(sums_ref[mine], steps_ref, begin + k)
                if k:
                    main = main - sub * ratio_ref[k - 1, mine]
                    values = values - sub * g_ref[k - 1, mine]
                inverse = 1.0 / main
                ratio_ref[k, mine] = sup * inverse
                g_ref[k, mine] = values * inverse

    split_shape = (ends_ref.shape[0], modes // ends_ref.shape[0], lanes)
    now = g_ref[total - 1]
    ends_ref[:, 1] = now.reshape(split_shape)
    for k in reversed(range(total - 1)):
        now = g_ref[k] - ratio_ref[k] * now
        g_ref[k] = now
    ends_ref[:, 0] = now.reshape(split_shape)


def eliminate(pieces, sums, bx, steps, count):
    t, rows, z = pieces[0].shape
    x = bx.shape[0]
    modes = rows * len(pieces)
    return pl.pallas_call(
        eliminate_body,
        in_specs=[SMEM, VMEM, SMEM, VMEM, VMEM] + [VMEM] * len(pieces),
        out_specs=[VMEM] * 2,
        out_shape=[array(t, modes, z), array(count, 2, modes // count, z)],
        scratch_shapes=[
            pltpu.VMEM((t, modes, z), f32),
            pltpu.VMEM((modes, z), f32),
            pltpu.VMEM((x, x), f32),
            pltpu.VMEM((x, 3 * x), bf16),
        ],
        compiler_params=params(),
        cost_estimate=cost(6 * t * modes * x * z, 8 * t * modes * z),
        name="eliminate",
    )(steps, *sums, bx, *pieces)


def return_body(steps_ref, ex_ref, ey_ref, ez_ref, bx_ref, g_ref, ends_ref, *refs):
    outs, (sol_ref, sums_ref, rows_ref, bx3_ref) = refs[:-4], refs[-4:]
    total, modes, lanes = g_ref.shape
    x = bx_ref.shape[0]
    span = x // len(outs)
    gather_rows(bx_ref, rows_ref, PEERS, 1)
    bx3_ref[...] = left3(rows_ref[...])
    fill_sums(ex_ref, ey_ref, ez_ref, sums_ref)
    begin = lax.axis_index("ta") * total
    before = ends_ref[:, 0].reshape(modes, lanes)
    after = ends_ref[:, 1].reshape(modes, lanes)
    eigen = sums_ref[...]
    ratios, values = [], []
    for k in range(total):
        main, sub, sup = row_terms(eigen, steps_ref, begin + k)
        inverse = 1.0 / (main - sub * ratios[-1] if k else main)
        ratios.append(sup * inverse)
        value = -(sub * inverse) * (values[-1] if k else before)
        if k == total - 1:
            value = value - ratios[-1] * after
        values.append(value)
    now = values[total - 1]
    sol_ref[total - 1] = g_ref[total - 1] + now
    for k in reversed(range(total - 1)):
        now = values[k] - ratios[k] * now
        sol_ref[k] = g_ref[k] + now

    for t in range(0, total, 2):
        for j in range(modes // x):
            cells = transform_pair(
                bx3_ref[...], [sol_ref[k, j * x : (j + 1) * x, :] for k in (t, t + 1)]
            )
            for k, cell in zip((t, t + 1), cells):
                for i, out in enumerate(outs):
                    out[k, j * span : (j + 1) * span, :] = cell[i * span : (i + 1) * span]


def return_x(g, ends, sums, bx, steps):
    t, modes, z = g.shape
    x, members = bx.shape[0], len(PEERS)
    return pl.pallas_call(
        return_body,
        in_specs=[SMEM, VMEM, SMEM, VMEM, VMEM, VMEM, VMEM],
        out_specs=[VMEM] * members,
        out_shape=[array(t, modes // members, z)] * members,
        scratch_shapes=[
            pltpu.VMEM((t, modes, z), f32),
            pltpu.VMEM((modes, z), f32),
            pltpu.VMEM((x, x), f32),
            pltpu.VMEM((x, 3 * x), bf16),
        ],
        compiler_params=params(),
        cost_estimate=cost(6 * t * modes * x * z, 8 * t * modes * z),
        name="return_x",
    )(steps, *sums, bx, g, ends)


def local(right_side, basis_x, basis_y, basis_z, eig_x, eig_y, eig_z, steps):
    rows = right_side.shape[0]
    count = lax.axis_size("ta")
    sums = (eig_x[None, :], eig_y, eig_z[None, :])
    share = basis_x.shape[0] * basis_y.shape[0] // (lax.axis_size("gx") * count)
    hbm = lambda value: pltpu.with_memory_space_constraint(value, pltpu.HBM)

    sent = forward_yz(hbm(right_side), hbm(basis_y), hbm(basis_z))
    moved = exchange(sent, PEERS)
    terms = list(reduced_terms(steps, sums, count, rows, share))
    moved[0], terms[0] = lax.optimization_barrier((moved[0], terms[0]))
    g, ends = eliminate(moved, sums, basis_x, steps, count)
    ends = lax.all_to_all(ends, "ta", 0, 0, tiled=True)
    ends = interface_solve(ends, terms)
    ends = lax.all_to_all(ends, "ta", 0, 0, tiled=True)
    moved = exchange(return_x(g, ends, sums, basis_x, steps), PEERS)
    return backward_yz(moved, basis_y, basis_z)


def solution(mesh):
    return jax.shard_map(
        local,
        mesh=mesh,
        in_specs=(P("ta", "gx", None, None), P(), P(), P(), P(), P(), P(), P()),
        out_specs=P("ta", "gx", None, None),
        check_vma=False,
    )
```

```python
from functools import partial

import jax
import jax.numpy as jnp
from jax import lax
from jax.experimental import pallas as pl
from jax.experimental.pallas import tpu as pltpu
from jax.sharding import PartitionSpec as P

f32, bf16 = jnp.float32, jnp.bfloat16
params = partial(pltpu.CompilerParams, vmem_limit_bytes=12 * 2**20)
VMEM = pl.BlockSpec(memory_space=pltpu.VMEM)
SMEM = pl.BlockSpec(memory_space=pltpu.SMEM)
ANY = pl.BlockSpec(memory_space=pl.ANY)

PEERS = ((0, 0), (2, 0), (2, 1), (1, 0), (3, 0), (1, 1), (3, 1), (0, 1))


def peer(member, members, place, sign):
    chips, core = place
    ring = members // 2
    far = lax.rem(member // 2 + (sign * chips) % ring, ring)
    own = lax.rem(member, 2)
    return far * 2 + (1 - own if core else own)


def exchange(pieces, peers):
    members = len(pieces)
    moved = [pieces[0]]
    for k in range(1, members):
        chips, core = peers[k]
        pairs = [(i, ((i // 2 + chips) * 2 + (i % 2 + core) % 2) % members) for i in range(members)]
        moved.append(lax.ppermute(pieces[k], "gx", pairs))
    return moved


def split(x):
    high = x.astype(bf16)
    return high, (x - high.astype(f32)).astype(bf16)


def left3(x):
    high, low = split(x)
    return jnp.concatenate([high, high, low], axis=1)


def right3(x):
    high, low = split(x)
    return jnp.concatenate([high, low, high], axis=0)


mm = partial(jnp.dot, preferred_element_type=f32)


def cost(flops, bytes_accessed):
    return pl.CostEstimate(flops=int(flops), bytes_accessed=int(bytes_accessed), transcendentals=0)


def array(*shape):
    return jax.ShapeDtypeStruct(shape, f32)


def gather_rows(source_ref, target_ref, peers, sign):
    members = len(peers)
    span = target_ref.shape[0] // members
    member = lax.axis_index("gx")
    for k, place in enumerate(peers):
        start = pl.multiple_of(peer(member, members, place, sign) * span, span)
        target_ref[k * span : (k + 1) * span] = source_ref[pl.ds(start, span), :]


def forward_body(x_any, by_any, bz_any, *refs):
    outs, refs = refs[: len(PEERS)], refs[len(PEERS) :]
    x_ref, by_ref, bz_ref, turn_ref, rows_ref, by3_ref, bz3_ref, x_sem, b_sem = refs
    total, rows, y, z = x_ref.shape
    span = y // len(outs)
    tables = [
        pltpu.make_async_copy(source, target, b_sem.at[k])
        for k, (source, target) in enumerate(((by_any, by_ref), (bz_any, bz_ref)))
    ]
    planes = [pltpu.make_async_copy(x_any.at[t], x_ref.at[t], x_sem.at[t]) for t in range(total)]
    for copy in tables + planes:
        copy.start()
    for copy in tables:
        copy.wait()
    turn_ref[...] = by_ref[...].T
    gather_rows(turn_ref, rows_ref, PEERS, 1)
    by3_ref[...] = left3(rows_ref[...])
    bz3_ref[...] = right3(bz_ref[...])

    for first in range(0, total, 4):
        times = range(first, first + 4)
        for t in times:
            planes[t].wait()
        vol = [mm(left3(x_ref[t].reshape(rows * y, z)), bz3_ref[...]) for t in times]
        for a in range(rows):
            plane = jnp.concatenate([v[a * y : (a + 1) * y] for v in vol], axis=1)
            plane = mm(by3_ref[...], right3(plane))
            for k, out in enumerate(outs):
                for i, t in enumerate(times):
                    out[t, pl.ds(a, span, stride=rows), :] = plane[
                        k * span : (k + 1) * span, i * z : (i + 1) * z
                    ]


def forward_yz(x, by, bz):
    t, a, y, z = x.shape
    members = len(PEERS)
    rows = a * y // members
    return pl.pallas_call(
        forward_body,
        in_specs=[ANY] * 3,
        out_specs=[VMEM] * members,
        out_shape=[array(t, rows, z)] * members,
        scratch_shapes=[
            pltpu.VMEM(x.shape, f32),
            pltpu.VMEM((y, y), f32),
            pltpu.VMEM((z, z), f32),
            pltpu.VMEM((y, y), f32),
            pltpu.VMEM((y, y), f32),
            pltpu.VMEM((y, 3 * y), bf16),
            pltpu.VMEM((3 * z, z), bf16),
            pltpu.SemaphoreType.DMA((t,)),
            pltpu.SemaphoreType.DMA((2,)),
        ],
        compiler_params=params(),
        cost_estimate=cost(6 * t * a * y * z * (y + z), 8 * t * a * y * z),
        name="forward_yz",
    )(x, by, bz)


def backward_body(by3_ref, bz3_ref, *refs):
    pieces, (out_any, out_ref, sem) = refs[: len(PEERS)], refs[len(PEERS) :]
    total, rows, y, z = out_ref.shape
    span = y // len(pieces)
    copies = []
    for first in range(0, total, 2):
        times = (first, first + 1)
        vol = []
        for a in range(rows):
            plane = jnp.concatenate(
                [
                    jnp.concatenate(
                        [piece[t, pl.ds(a, span, stride=rows), :] for piece in pieces], axis=0
                    )
                    for t in times
                ],
                axis=1,
            )
            vol.append(mm(by3_ref[...], right3(plane)))
        for i, t in enumerate(times):
            flat = jnp.concatenate([v[:, i * z : (i + 1) * z] for v in vol], axis=0)
            out_ref[t] = mm(left3(flat), bz3_ref[...]).reshape(rows, y, z)
        for t in times:
            copies.append(pltpu.make_async_copy(out_ref.at[t], out_any.at[t], sem.at[t]))
            copies[-1].start()
    for copy in copies:
        copy.wait()


def backward_yz(pieces, by3, bz3):
    members = len(pieces)
    y, z = by3.shape[0], bz3.shape[1]
    t, rows = pieces[0].shape[:2]
    a = rows * members // y
    return pl.pallas_call(
        backward_body,
        in_specs=[VMEM] * (2 + members),
        out_specs=ANY,
        out_shape=array(t, a, y, z),
        scratch_shapes=[pltpu.VMEM((t, a, y, z), f32), pltpu.SemaphoreType.DMA((t,))],
        compiler_params=params(),
        cost_estimate=cost(6 * t * a * y * z * (y + z), 8 * t * a * y * z),
        name="backward_yz",
    )(by3, bz3, *pieces)


def length(steps_ref, at):
    total = steps_ref.shape[0]
    here = steps_ref[jnp.minimum(at, total - 1)] / total
    return jnp.where(at < total, here, 0.0)


def row_terms(eigen, steps_ref, at):
    now, then = length(steps_ref, at), length(steps_ref, at + 1)
    closing = jnp.where(at == steps_ref.shape[0] - 1, 0.5, 0.0)
    main = eigen * ((now + then) / 3.0) + closing
    sub = eigen * (now / 6.0) - 0.5
    sup = eigen * (then / 6.0) + 0.5
    return main, sub, sup


def mode_sums(ex_ref, ey_ref, ez_ref, j):
    x, z = ex_ref.shape[1], ez_ref.shape[1]
    along_x = jnp.broadcast_to(ex_ref[...], (z, x)).T
    return (along_x + ey_ref[j]) + ez_ref[...]


def prepare_body(steps_ref, ex_ref, ey_ref, ez_ref, bx_ref, by_ref, bz_ref, *refs):
    inv_ref, mul_ref, ratio_ref, v_ref, w_ref, bx3_ref, bx3_back_ref, by3_ref, bz3_ref = refs[:9]
    sums_ref, turn_ref, rows_ref = refs[9:]
    total, modes, lanes = inv_ref.shape
    x, members = ex_ref.shape[1], len(PEERS)
    gather_rows(bx_ref, rows_ref, PEERS, -1)
    bx3_ref[...] = left3(rows_ref[...].T)
    gather_rows(bx_ref, rows_ref, PEERS, 1)
    bx3_back_ref[...] = left3(rows_ref[...])
    turn_ref[...] = by_ref[...].T
    gather_rows(turn_ref, rows_ref, PEERS, -1)
    by3_ref[...] = left3(rows_ref[...].T)
    bz3_ref[...] = right3(bz_ref[...].T)

    span = ey_ref.shape[0] // members
    member = lax.axis_index("gx")
    for j in range(span):
        sums_ref[j * x : (j + 1) * x] = mode_sums(ex_ref, ey_ref, ez_ref, member * span + j)
    begin = lax.axis_index("ta") * total
    size = 32

    def block(n, carry):
        mine = pl.ds(pl.multiple_of(n * size, size), size)
        eigen = sums_ref[mine, :]
        ratios, fronts = [], []
        for k in range(total):
            main, sub, sup = row_terms(eigen, steps_ref, begin + k)
            inverse = 1.0 / (main - sub * ratios[-1] if k else main)
            factor = sub * inverse
            ratios.append(sup * inverse)
            fronts.append(-factor * fronts[-1] if k else factor)
            inv_ref[k, mine, :] = inverse
            mul_ref[k, mine, :] = factor
            ratio_ref[k, mine, :] = ratios[-1]
        low, last = fronts[-1], ratios[-1]
        v_ref[total - 1, mine, :] = low
        w_ref[total - 1, mine, :] = last
        for k in reversed(range(total - 1)):
            low = fronts[k] - ratios[k] * low
            last = -ratios[k] * last
            v_ref[k, mine, :] = low
            w_ref[k, mine, :] = last
        return carry

    lax.fori_loop(0, modes // size, block, 0)


def prepare(steps, sums, bx, by, bz, rows):
    x, y, z = bx.shape[0], by.shape[0], bz.shape[0]
    modes = x * y // len(PEERS)
    table = lambda *shape: jax.ShapeDtypeStruct(shape, bf16)
    return pl.pallas_call(
        prepare_body,
        in_specs=[SMEM, VMEM, SMEM, VMEM, VMEM, VMEM, VMEM],
        out_specs=[VMEM] * 9,
        out_shape=[array(rows, modes, z)] * 5
        + [table(x, 3 * x), table(x, 3 * x), table(y, 3 * y), table(3 * z, z)],
        scratch_shapes=[
            pltpu.VMEM((modes, z), f32),
            pltpu.VMEM((y, y), f32),
            pltpu.VMEM((x, x), f32),
        ],
        compiler_params=params(),
        cost_estimate=cost(30 * rows * modes * z, 20 * rows * modes * z),
        name="prepare",
    )(steps, *sums, bx, by, bz)


def reduced_body(rows, steps_ref, ex_ref, ey_ref, ez_ref, cl_ref, e_ref, a_ref, k_ref, b_ref, q_ref, sums_ref):
    count, share = cl_ref.shape[:2]
    x, span = ex_ref.shape[1], ey_ref.shape[0] // len(PEERS)
    first = lax.axis_index("ta") * share
    sums_ref[...] = mode_sums(ex_ref, ey_ref, ez_ref, lax.axis_index("gx") * span + first // x)
    eigen = sums_ref[pl.ds(pl.multiple_of(lax.rem(first, x), share), share), :]

    def block(j, carry):
        inverses, subs, ratios = [], [], []
        for k in range(rows):
            main, sub, sup = row_terms(eigen, steps_ref, j * rows + k)
            inverse = 1.0 / (main - sub * ratios[-1] if k else main)
            inverses.append(inverse)
            subs.append(sub)
            ratios.append(sup * inverse)
        front = subs[0] * inverses[0]
        fronts = [front]
        for k in range(1, rows):
            front = -(subs[k] * inverses[k]) * front
            fronts.append(front)
        last = ratios[rows - 1]
        low = fronts[rows - 1]
        cl_ref[j] = low
        e_ref[j] = last
        for k in reversed(range(rows - 1)):
            low = fronts[k] - ratios[k] * low
            last = -ratios[k] * last
        a_ref[j] = low
        b_ref[j] = last
        return carry

    lax.fori_loop(0, count, block, 0, unroll=4)

    def sweep(j, q_before):
        v_last, w_last, v_first, w_first = cl_ref[j], e_ref[j], a_ref[j], b_ref[j]
        scale = 1.0 / (1.0 - v_first * q_before)
        back = w_first * scale
        q_now = w_last + v_last * q_before * back
        e_now = v_last * scale
        cl_ref[j] = e_now * q_before
        e_ref[j] = e_now
        a_ref[j] = scale
        k_ref[j] = v_first * scale
        b_ref[j] = back
        q_ref[j] = q_now
        return q_now

    lax.fori_loop(0, count, sweep, jnp.zeros_like(eigen))


def reduced_terms(steps, sums, count, rows, share):
    x, z = sums[0].shape[1], sums[2].shape[1]
    return pl.pallas_call(
        partial(reduced_body, rows),
        in_specs=[SMEM, VMEM, SMEM, VMEM],
        out_specs=[VMEM] * 6,
        out_shape=[array(count, share, z)] * 6,
        scratch_shapes=[pltpu.VMEM((x, z), f32)],
        compiler_params=params(),
        cost_estimate=cost(40 * rows * count * share * z, 24 * count * share * z),
        name="reduced_terms",
    )(steps, *sums)


def interface_body(g_ref, cl_ref, e_ref, a_ref, k_ref, b_ref, q_ref, out_ref, fh_ref):
    count = g_ref.shape[0]
    zero = jnp.zeros(g_ref.shape[2:], f32)

    def down(j, before):
        first, last = g_ref[j, 0], g_ref[j, 1]
        out_ref[j, 0] = before
        fh_ref[j] = a_ref[j] * first - k_ref[j] * before
        return (last + cl_ref[j] * first) - e_ref[j] * before

    lax.fori_loop(0, count, down, zero, unroll=8)

    def up(i, after):
        j = count - 1 - i
        out_ref[j, 1] = after

        @pl.when(j < count - 1)
        def _():
            out_ref[j + 1, 0] = out_ref[j + 1, 0] - q_ref[j] * after

        return fh_ref[j] - b_ref[j] * after

    lax.fori_loop(0, count, up, zero, unroll=8)


def interface_solve(g, terms):
    return pl.pallas_call(
        interface_body,
        in_specs=[VMEM] * 7,
        out_specs=VMEM,
        out_shape=array(*g.shape),
        scratch_shapes=[pltpu.VMEM(g.shape[:1] + g.shape[2:], f32)],
        compiler_params=params(),
        cost_estimate=cost(6 * g.size, 20 * g.size),
        name="interface_solve",
    )(g, *terms)


def transform_pair(table, planes):
    lanes = planes[0].shape[1]
    both = mm(table, right3(jnp.concatenate(planes, axis=1)))
    return both[:, :lanes], both[:, lanes:]


def eliminate_body(bx3_ref, inv_ref, mul_ref, ratio_ref, *refs):
    pieces, (g_ref, ends_ref) = refs[:-2], refs[-2:]
    total, modes, lanes = g_ref.shape
    x = bx3_ref.shape[0]
    span = x // len(pieces)
    for t in range(0, total, 2):
        for j in range(modes // x):
            mine = slice(j * x, (j + 1) * x)
            spectral = transform_pair(
                bx3_ref[...],
                [
                    jnp.concatenate([piece[k, j * span : (j + 1) * span, :] for piece in pieces], axis=0)
                    for k in (t, t + 1)
                ],
            )
            for k, values in zip((t, t + 1), spectral):
                values = values * inv_ref[k, mine]
                g_ref[k, mine] = values - mul_ref[k, mine] * g_ref[k - 1, mine] if k else values

    split_shape = (ends_ref.shape[0], modes // ends_ref.shape[0], lanes)
    now = g_ref[total - 1]
    ends_ref[:, 1] = now.reshape(split_shape)
    for k in reversed(range(total - 1)):
        now = g_ref[k] - ratio_ref[k] * now
        g_ref[k] = now
    ends_ref[:, 0] = now.reshape(split_shape)


def eliminate(pieces, bx3, factors, count):
    t, rows, z = pieces[0].shape
    x = bx3.shape[0]
    modes = rows * len(pieces)
    return pl.pallas_call(
        eliminate_body,
        in_specs=[VMEM] * (4 + len(pieces)),
        out_specs=[VMEM] * 2,
        out_shape=[array(t, modes, z), array(count, 2, modes // count, z)],
        compiler_params=params(),
        cost_estimate=cost(6 * t * modes * x * z, 20 * t * modes * z),
        name="eliminate",
    )(bx3, *factors, *pieces)


def return_body(bx3_ref, v_ref, w_ref, g_ref, ends_ref, *outs):
    total, modes, lanes = g_ref.shape
    x = bx3_ref.shape[0]
    span = x // len(outs)
    share = modes // ends_ref.shape[0]
    for j in range(modes // x):
        mine = slice(j * x, (j + 1) * x)
        owners = slice(j * x // share, (j + 1) * x // share)
        before = ends_ref[owners, 0].reshape(x, lanes)
        after = ends_ref[owners, 1].reshape(x, lanes)
        for t in range(0, total, 2):
            cells = transform_pair(
                bx3_ref[...],
                [
                    g_ref[k, mine] - v_ref[k, mine] * before - w_ref[k, mine] * after
                    for k in (t, t + 1)
                ],
            )
            for k, cell in zip((t, t + 1), cells):
                for i, out in enumerate(outs):
                    out[k, j * span : (j + 1) * span, :] = cell[i * span : (i + 1) * span]


def return_x(g, ends, bx3, v, w):
    t, modes, z = g.shape
    x, members = bx3.shape[0], len(PEERS)
    return pl.pallas_call(
        return_body,
        in_specs=[VMEM] * 5,
        out_specs=[VMEM] * members,
        out_shape=[array(t, modes // members, z)] * members,
        compiler_params=params(),
        cost_estimate=cost(6 * t * modes * x * z, 16 * t * modes * z),
        name="return_x",
    )(bx3, v, w, g, ends)


def local(right_side, basis_x, basis_y, basis_z, eig_x, eig_y, eig_z, steps):
    rows = right_side.shape[0]
    count = lax.axis_size("ta")
    sums = (eig_x[None, :], eig_y, eig_z[None, :])
    share = basis_x.shape[0] * basis_y.shape[0] // (lax.axis_size("gx") * count)
    hbm = lambda value: pltpu.with_memory_space_constraint(value, pltpu.HBM)

    sent = forward_yz(hbm(right_side), hbm(basis_y), hbm(basis_z))
    moved = exchange(sent, PEERS)
    terms = list(reduced_terms(steps, sums, count, rows, share))
    *factors, v, w, bx3, bx3_back, by3, bz3 = prepare(steps, sums, basis_x, basis_y, basis_z, rows)
    moved[0], terms[0], bx3 = lax.optimization_barrier((moved[0], terms[0], bx3))
    g, ends = eliminate(moved, bx3, factors, count)
    ends = lax.all_to_all(ends, "ta", 0, 0, tiled=True)
    ends = interface_solve(ends, terms)
    ends = lax.all_to_all(ends, "ta", 0, 0, tiled=True)
    moved = exchange(return_x(g, ends, bx3_back, v, w), PEERS)
    return backward_yz(moved, by3, bz3)


def solution(mesh):
    return jax.shard_map(
        local,
        mesh=mesh,
        in_specs=(P("ta", "gx", None, None), P(), P(), P(), P(), P(), P(), P()),
        out_specs=P("ta", "gx", None, None),
        check_vma=False,
    )
```

```python
from functools import partial

import jax
import jax.numpy as jnp
from jax import lax
from jax.experimental import pallas as pl
from jax.experimental.pallas import tpu as pltpu
from jax.sharding import PartitionSpec as P

f32, bf16 = jnp.float32, jnp.bfloat16
params = partial(pltpu.CompilerParams, vmem_limit_bytes=12 * 2**20)
VMEM = pl.BlockSpec(memory_space=pltpu.VMEM)
SMEM = pl.BlockSpec(memory_space=pltpu.SMEM)
ANY = pl.BlockSpec(memory_space=pl.ANY)

PEERS = ((0, 0), (2, 0), (2, 1), (1, 0), (3, 0), (1, 1), (3, 1), (0, 1))


def peer(member, members, place, sign):
    chips, core = place
    ring = members // 2
    far = lax.rem(member // 2 + (sign * chips) % ring, ring)
    own = lax.rem(member, 2)
    return far * 2 + (1 - own if core else own)


def send(piece, place, members):
    chips, core = place
    pairs = [(i, ((i // 2 + chips) * 2 + (i % 2 + core) % 2) % members) for i in range(members)]
    return lax.ppermute(piece, "gx", pairs)


def exchange(pieces):
    moved = [send(piece, place, len(PEERS)) for piece, place in zip(pieces[1:], PEERS[1:])]
    return [pieces[0]] + moved


def split(x):
    high = x.astype(bf16)
    return high, (x - high.astype(f32)).astype(bf16)


def left3(x):
    high, low = split(x)
    return jnp.concatenate([high, high, low], axis=1)


def right3(x):
    high, low = split(x)
    return jnp.concatenate([high, low, high], axis=0)


mm = partial(jnp.dot, preferred_element_type=f32)


def cost(flops, bytes_accessed):
    return pl.CostEstimate(flops=int(flops), bytes_accessed=int(bytes_accessed), transcendentals=0)


def array(*shape):
    return jax.ShapeDtypeStruct(shape, f32)


def gather_rows(source_ref, target_ref, peers, sign):
    span = target_ref.shape[0] // len(peers)
    member = lax.axis_index("gx")
    for k, place in enumerate(peers):
        start = pl.multiple_of(peer(member, len(PEERS), place, sign) * span, span)
        target_ref[k * span : (k + 1) * span] = source_ref[pl.ds(start, span), :]


def forward_body(peers, x_any, by_any, bz_any, *refs):
    outs, refs = refs[: len(peers)], refs[len(peers) :]
    x_ref, by_ref, bz_ref, turn_ref, rows_ref, by3_ref, bz3_ref, x_sem, b_sem = refs
    total, rows, y, z = x_ref.shape
    size = outs[0].shape[1]
    span = size // rows
    tables = [
        pltpu.make_async_copy(source, target, b_sem.at[k])
        for k, (source, target) in enumerate(((by_any, by_ref), (bz_any, bz_ref)))
    ]
    planes = [pltpu.make_async_copy(x_any.at[t], x_ref.at[t], x_sem.at[t]) for t in range(total)]
    for copy in planes + tables:
        copy.start()
    for copy in planes + tables:
        copy.wait()
    turn_ref[...] = by_ref[...].T
    gather_rows(turn_ref, rows_ref, peers, 1)
    by3_ref[...] = left3(rows_ref[...])
    bz3_ref[...] = right3(bz_ref[...])

    vol = [mm(left3(x_ref[t].reshape(rows * y, z)), bz3_ref[...]) for t in range(total)]
    for first in range(0, total, 4):
        times = range(first, first + 4)
        for a in range(rows):
            plane = jnp.concatenate([vol[t][a * y : (a + 1) * y] for t in times], axis=1)
            plane = mm(by3_ref[...], right3(plane))
            for k, out in enumerate(outs):
                for i, t in enumerate(times):
                    out[t, pl.ds(a, span, stride=rows), :] = plane[
                        k * span : (k + 1) * span, i * z : (i + 1) * z
                    ]


def forward_yz(x, by, bz, peers):
    t, a, y, z = x.shape
    span = y // len(PEERS)
    return pl.pallas_call(
        partial(forward_body, peers),
        in_specs=[ANY] * 3,
        out_specs=[VMEM] * len(peers),
        out_shape=[array(t, a * span, z)] * len(peers),
        scratch_shapes=[
            pltpu.VMEM(x.shape, f32),
            pltpu.VMEM((y, y), f32),
            pltpu.VMEM((z, z), f32),
            pltpu.VMEM((y, y), f32),
            pltpu.VMEM((len(peers) * span, y), f32),
            pltpu.VMEM((len(peers) * span, 3 * y), bf16),
            pltpu.VMEM((3 * z, z), bf16),
            pltpu.SemaphoreType.DMA((t,)),
            pltpu.SemaphoreType.DMA((2,)),
        ],
        compiler_params=params(),
        cost_estimate=cost(6 * t * a * len(peers) * span * z * (y + z), 8 * t * a * y * z),
        name="forward_yz",
    )(x, by, bz)


def backward_planes(times, rows, by3_ref, bz3_ref, pieces, mid_ref):
    size, z = pieces[0].shape[1:]
    span = size // rows
    for t in times:
        flat = jnp.concatenate([piece[t] for piece in pieces], axis=0)
        mid_ref[t] = mm(left3(flat), bz3_ref[...])
    for a in range(rows):
        plane = [
            jnp.concatenate(
                [mid_ref[t, pl.ds(k * size + a, span, stride=rows), :] for k in range(len(pieces))],
                axis=0,
            )
            for t in times
        ]
        plane = mm(by3_ref[...], right3(jnp.concatenate(plane, axis=1)))
        for i, t in enumerate(times):
            yield t, a, plane[:, i * z : (i + 1) * z]


def backward_early_body(by3_ref, bz3_ref, *refs):
    pieces, (out_ref, mid_ref) = refs[:-2], refs[-2:]
    total, rows = out_ref.shape[:2]
    for first in range(0, total, 2):
        times = (first, first + 1)
        for t, a, plane in backward_planes(times, rows, by3_ref, bz3_ref, pieces, mid_ref):
            out_ref[t, a] = plane


def backward_late_body(by3_ref, bz3_ref, early_ref, *refs):
    pieces, (out_any, out_ref, mid_ref, sem) = refs[:-4], refs[-4:]
    total, rows = out_ref.shape[:2]
    copies = []
    for first in range(0, total, 2):
        times = (first, first + 1)
        for t, a, plane in backward_planes(times, rows, by3_ref, bz3_ref, pieces, mid_ref):
            out_ref[t, a] = early_ref[t, a] + plane
        for t in times:
            copies.append(pltpu.make_async_copy(out_ref.at[t], out_any.at[t], sem.at[t]))
            copies[-1].start()
    for copy in copies:
        copy.wait()


def backward_yz(pieces, by3, bz3, early=()):
    y, z = by3.shape[0], bz3.shape[1]
    t, size = pieces[0].shape[:2]
    a = size * len(PEERS) // y
    mid = pltpu.VMEM((t, len(pieces) * size, z), f32)
    scratch = [pltpu.VMEM((t, a, y, z), f32), mid, pltpu.SemaphoreType.DMA((t,))]
    return pl.pallas_call(
        backward_late_body if early else backward_early_body,
        in_specs=[VMEM] * (2 + len(early) + len(pieces)),
        out_specs=ANY if early else VMEM,
        out_shape=array(t, a, y, z),
        scratch_shapes=scratch if early else [mid],
        compiler_params=params(),
        cost_estimate=cost(6 * t * size * len(pieces) * z * (y + z), 8 * t * a * y * z),
        name="backward_yz",
    )(by3, bz3, *early, *pieces)


def length(steps_ref, at):
    total = steps_ref.shape[0]
    here = steps_ref[jnp.minimum(at, total - 1)] / total
    return jnp.where(at < total, here, 0.0)


def row_terms(eigen, steps_ref, at):
    now, then = length(steps_ref, at), length(steps_ref, at + 1)
    closing = jnp.where(at == steps_ref.shape[0] - 1, 0.5, 0.0)
    main = eigen * ((now + then) / 3.0) + closing
    sub = eigen * (now / 6.0) - 0.5
    sup = eigen * (then / 6.0) + 0.5
    return main, sub, sup


def mode_sums(ex_ref, ey_ref, ez_ref, j):
    x, z = ex_ref.shape[1], ez_ref.shape[1]
    along_x = jnp.broadcast_to(ex_ref[...], (z, x)).T
    return (along_x + ey_ref[j]) + ez_ref[...]


def prepare_body(steps_ref, ex_ref, ey_ref, ez_ref, bx_ref, by_ref, bz_ref, *refs):
    inv_ref, mul_ref, ratio_ref, v_ref, w_ref, bx3_ref, bx3_back_ref, *by3_refs, bz3_ref = refs[:10]
    sums_ref, turn_ref, rows_ref = refs[10:]
    total, modes, lanes = inv_ref.shape
    x, members = ex_ref.shape[1], len(PEERS)
    gather_rows(bx_ref, rows_ref, PEERS, -1)
    bx3_ref[...] = left3(rows_ref[...].T)
    gather_rows(bx_ref, rows_ref, PEERS, 1)
    bx3_back_ref[...] = left3(rows_ref[...])
    turn_ref[...] = by_ref[...].T
    gather_rows(turn_ref, rows_ref, PEERS, -1)
    half = rows_ref.shape[0] // 2
    for k, ref in enumerate(by3_refs):
        ref[...] = left3(rows_ref[k * half : (k + 1) * half].T)
    bz3_ref[...] = right3(bz_ref[...].T)

    span = ey_ref.shape[0] // members
    member = lax.axis_index("gx")
    for j in range(span):
        sums_ref[j * x : (j + 1) * x] = mode_sums(ex_ref, ey_ref, ez_ref, member * span + j)
    begin = lax.axis_index("ta") * total
    size = 32

    def block(n, carry):
        mine = pl.ds(pl.multiple_of(n * size, size), size)
        eigen = sums_ref[mine, :]
        ratios, fronts = [], []
        for k in range(total):
            main, sub, sup = row_terms(eigen, steps_ref, begin + k)
            inverse = 1.0 / (main - sub * ratios[-1] if k else main)
            factor = sub * inverse
            ratios.append(sup * inverse)
            fronts.append(-factor * fronts[-1] if k else factor)
            inv_ref[k, mine, :] = inverse
            mul_ref[k, mine, :] = factor
            ratio_ref[k, mine, :] = ratios[-1]
        low, last = fronts[-1], ratios[-1]
        v_ref[total - 1, mine, :] = low
        w_ref[total - 1, mine, :] = last
        for k in reversed(range(total - 1)):
            low = fronts[k] - ratios[k] * low
            last = -ratios[k] * last
            v_ref[k, mine, :] = low
            w_ref[k, mine, :] = last
        return carry

    lax.fori_loop(0, modes // size, block, 0)


def prepare(steps, sums, bx, by, bz, rows):
    x, y, z = bx.shape[0], by.shape[0], bz.shape[0]
    modes = x * y // len(PEERS)
    table = lambda *shape: jax.ShapeDtypeStruct(shape, bf16)
    return pl.pallas_call(
        prepare_body,
        in_specs=[SMEM, VMEM, SMEM, VMEM, VMEM, VMEM, VMEM],
        out_specs=[VMEM] * 10,
        out_shape=[array(rows, modes, z)] * 5
        + [table(x, 3 * x)] * 2
        + [table(y, 3 * y // 2)] * 2
        + [table(3 * z, z)],
        scratch_shapes=[
            pltpu.VMEM((modes, z), f32),
            pltpu.VMEM((y, y), f32),
            pltpu.VMEM((x, x), f32),
        ],
        compiler_params=params(),
        cost_estimate=cost(30 * rows * modes * z, 20 * rows * modes * z),
        name="prepare",
    )(steps, *sums, bx, by, bz)


def reduced_body(rows, steps_ref, ex_ref, ey_ref, ez_ref, cl_ref, e_ref, a_ref, k_ref, b_ref, q_ref, sums_ref):
    count, share = cl_ref.shape[:2]
    x, span = ex_ref.shape[1], ey_ref.shape[0] // len(PEERS)
    first = lax.axis_index("ta") * share
    sums_ref[...] = mode_sums(ex_ref, ey_ref, ez_ref, lax.axis_index("gx") * span + first // x)
    eigen = sums_ref[pl.ds(pl.multiple_of(lax.rem(first, x), share), share), :]

    def block(j, carry):
        inverses, subs, ratios = [], [], []
        for k in range(rows):
            main, sub, sup = row_terms(eigen, steps_ref, j * rows + k)
            inverse = 1.0 / (main - sub * ratios[-1] if k else main)
            inverses.append(inverse)
            subs.append(sub)
            ratios.append(sup * inverse)
        front = subs[0] * inverses[0]
        fronts = [front]
        for k in range(1, rows):
            front = -(subs[k] * inverses[k]) * front
            fronts.append(front)
        last = ratios[rows - 1]
        low = fronts[rows - 1]
        cl_ref[j] = low
        e_ref[j] = last
        for k in reversed(range(rows - 1)):
            low = fronts[k] - ratios[k] * low
            last = -ratios[k] * last
        a_ref[j] = low
        b_ref[j] = last
        return carry

    lax.fori_loop(0, count, block, 0, unroll=4)

    def sweep(j, q_before):
        v_last, w_last, v_first, w_first = cl_ref[j], e_ref[j], a_ref[j], b_ref[j]
        scale = 1.0 / (1.0 - v_first * q_before)
        back = w_first * scale
        q_now = w_last + v_last * q_before * back
        e_now = v_last * scale
        cl_ref[j] = e_now * q_before
        e_ref[j] = e_now
        a_ref[j] = scale
        k_ref[j] = v_first * scale
        b_ref[j] = back
        q_ref[j] = q_now
        return q_now

    lax.fori_loop(0, count, sweep, jnp.zeros_like(eigen))


def reduced_terms(steps, sums, count, rows, share):
    x, z = sums[0].shape[1], sums[2].shape[1]
    return pl.pallas_call(
        partial(reduced_body, rows),
        in_specs=[SMEM, VMEM, SMEM, VMEM],
        out_specs=[VMEM] * 6,
        out_shape=[array(count, share, z)] * 6,
        scratch_shapes=[pltpu.VMEM((x, z), f32)],
        compiler_params=params(),
        cost_estimate=cost(40 * rows * count * share * z, 24 * count * share * z),
        name="reduced_terms",
    )(steps, *sums)


def interface_body(g_ref, cl_ref, e_ref, a_ref, k_ref, b_ref, q_ref, out_ref, fh_ref):
    count = g_ref.shape[0]
    zero = jnp.zeros(g_ref.shape[2:], f32)

    def down(j, before):
        first, last = g_ref[j, 0], g_ref[j, 1]
        out_ref[j, 0] = before
        fh_ref[j] = a_ref[j] * first - k_ref[j] * before
        return (last + cl_ref[j] * first) - e_ref[j] * before

    lax.fori_loop(0, count, down, zero, unroll=8)

    def up(i, after):
        j = count - 1 - i
        out_ref[j, 1] = after

        @pl.when(j < count - 1)
        def _():
            out_ref[j + 1, 0] = out_ref[j + 1, 0] - q_ref[j] * after

        return fh_ref[j] - b_ref[j] * after

    lax.fori_loop(0, count, up, zero, unroll=8)


def interface_solve(g, terms):
    return pl.pallas_call(
        interface_body,
        in_specs=[VMEM] * 7,
        out_specs=VMEM,
        out_shape=array(*g.shape),
        scratch_shapes=[pltpu.VMEM(g.shape[:1] + g.shape[2:], f32)],
        compiler_params=params(),
        cost_estimate=cost(6 * g.size, 20 * g.size),
        name="interface_solve",
    )(g, *terms)


def transform_pair(table, planes):
    lanes = planes[0].shape[1]
    both = mm(table, right3(jnp.concatenate(planes, axis=1)))
    return both[:, :lanes], both[:, lanes:]


def eliminate_body(bx3_ref, inv_ref, mul_ref, ratio_ref, *refs):
    pieces, (g_ref, ends_ref) = refs[:-2], refs[-2:]
    total, modes, lanes = g_ref.shape
    x = bx3_ref.shape[0]
    span = x // len(pieces)
    for t in range(0, total, 2):
        for j in range(modes // x):
            mine = slice(j * x, (j + 1) * x)
            spectral = transform_pair(
                bx3_ref[...],
                [
                    jnp.concatenate([piece[k, j * span : (j + 1) * span, :] for piece in pieces], axis=0)
                    for k in (t, t + 1)
                ],
            )
            for k, values in zip((t, t + 1), spectral):
                values = values * inv_ref[k, mine]
                g_ref[k, mine] = values - mul_ref[k, mine] * g_ref[k - 1, mine] if k else values

    split_shape = (ends_ref.shape[0], modes // ends_ref.shape[0], lanes)
    now = g_ref[total - 1]
    ends_ref[:, 1] = now.reshape(split_shape)
    for k in reversed(range(total - 1)):
        now = g_ref[k] - ratio_ref[k] * now
        g_ref[k] = now
    ends_ref[:, 0] = now.reshape(split_shape)


def eliminate(pieces, bx3, factors, count):
    t, rows, z = pieces[0].shape
    x = bx3.shape[0]
    modes = rows * len(pieces)
    return pl.pallas_call(
        eliminate_body,
        in_specs=[VMEM] * (4 + len(pieces)),
        out_specs=[VMEM] * 2,
        out_shape=[array(t, modes, z), array(count, 2, modes // count, z)],
        compiler_params=params(),
        cost_estimate=cost(6 * t * modes * x * z, 20 * t * modes * z),
        name="eliminate",
    )(bx3, *factors, *pieces)


def return_body(bx3_ref, v_ref, w_ref, g_ref, ends_ref, *outs):
    total, modes, lanes = g_ref.shape
    x = bx3_ref.shape[0]
    span = x // len(outs)
    share = modes // ends_ref.shape[0]
    for j in range(modes // x):
        mine = slice(j * x, (j + 1) * x)
        owners = slice(j * x // share, (j + 1) * x // share)
        before = ends_ref[owners, 0].reshape(x, lanes)
        after = ends_ref[owners, 1].reshape(x, lanes)
        for t in range(0, total, 2):
            cells = transform_pair(
                bx3_ref[...],
                [
                    g_ref[k, mine] - v_ref[k, mine] * before - w_ref[k, mine] * after
                    for k in (t, t + 1)
                ],
            )
            for k, cell in zip((t, t + 1), cells):
                for i, out in enumerate(outs):
                    out[k, j * span : (j + 1) * span, :] = cell[i * span : (i + 1) * span]


def return_x(g, ends, bx3, v, w):
    t, modes, z = g.shape
    x, members = bx3.shape[0], len(PEERS)
    return pl.pallas_call(
        return_body,
        in_specs=[VMEM] * 5,
        out_specs=[VMEM] * members,
        out_shape=[array(t, modes // members, z)] * members,
        compiler_params=params(),
        cost_estimate=cost(6 * t * modes * x * z, 16 * t * modes * z),
        name="return_x",
    )(bx3, v, w, g, ends)


def local(right_side, basis_x, basis_y, basis_z, eig_x, eig_y, eig_z, steps):
    rows = right_side.shape[0]
    count = lax.axis_size("ta")
    sums = (eig_x[None, :], eig_y, eig_z[None, :])
    share = basis_x.shape[0] * basis_y.shape[0] // (lax.axis_size("gx") * count)
    hbm = lambda value: pltpu.with_memory_space_constraint(value, pltpu.HBM)

    given = (hbm(right_side), hbm(basis_y), hbm(basis_z))
    far, near = PEERS[1:5], PEERS[:1] + PEERS[5:]
    sent = forward_yz(*given, far)
    rest = forward_yz(*given, near)
    moved = exchange([rest[0], *sent, *rest[1:]])
    terms = list(reduced_terms(steps, sums, count, rows, share))
    *factors, v, w, bx3, bx3_back, by3_early, by3_late, bz3 = prepare(steps, sums, basis_x, basis_y, basis_z, rows)
    moved[0], terms[0], bx3 = lax.optimization_barrier((moved[0], terms[0], bx3))
    g, ends = eliminate(moved, bx3, factors, count)
    ends = lax.all_to_all(ends, "ta", 0, 0, tiled=True)
    ends = interface_solve(ends, terms)
    ends = lax.all_to_all(ends, "ta", 0, 0, tiled=True)
    moved = exchange(return_x(g, ends, bx3_back, v, w))
    early = backward_yz(moved[:4], by3_early, bz3)
    return backward_yz(moved[4:], by3_late, bz3, (early,))


def solution(mesh):
    return jax.shard_map(
        local,
        mesh=mesh,
        in_specs=(P("ta", "gx", None, None), P(), P(), P(), P(), P(), P(), P()),
        out_specs=P("ta", "gx", None, None),
        check_vma=False,
    )
```

```python
from functools import partial

import jax
import jax.numpy as jnp
from jax import lax
from jax.experimental import pallas as pl
from jax.experimental.pallas import tpu as pltpu
from jax.sharding import PartitionSpec as P

f32, bf16 = jnp.float32, jnp.bfloat16
params = partial(pltpu.CompilerParams, vmem_limit_bytes=12 * 2**20)
VMEM = pl.BlockSpec(memory_space=pltpu.VMEM)
SMEM = pl.BlockSpec(memory_space=pltpu.SMEM)
ANY = pl.BlockSpec(memory_space=pl.ANY)

PEERS = ((0, 0), (2, 0), (2, 1), (1, 0), (3, 0), (1, 1), (3, 1), (0, 1))


def peer(member, members, place, sign):
    chips, core = place
    ring = members // 2
    far = lax.rem(member // 2 + (sign * chips) % ring, ring)
    own = lax.rem(member, 2)
    return far * 2 + (1 - own if core else own)


def send(piece, place, members):
    chips, core = place
    pairs = [(i, ((i // 2 + chips) * 2 + (i % 2 + core) % 2) % members) for i in range(members)]
    return lax.ppermute(piece, "gx", pairs)


def exchange(pieces):
    moved = [send(piece, place, len(PEERS)) for piece, place in zip(pieces[1:], PEERS[1:])]
    return [pieces[0]] + moved


def split(x):
    high = x.astype(bf16)
    return high, (x - high.astype(f32)).astype(bf16)


def left3(x):
    high, low = split(x)
    return jnp.concatenate([high, high, low], axis=1)


def right3(x):
    high, low = split(x)
    return jnp.concatenate([high, low, high], axis=0)


mm = partial(jnp.dot, preferred_element_type=f32)


def cost(flops, bytes_accessed):
    return pl.CostEstimate(flops=int(flops), bytes_accessed=int(bytes_accessed), transcendentals=0)


def array(*shape):
    return jax.ShapeDtypeStruct(shape, f32)


FAR, NEAR = PEERS[1:5], PEERS[:1] + PEERS[5:]


def gather_rows(source_ref, target_ref, peers, sign):
    span = target_ref.shape[0] // len(peers)
    member = lax.axis_index("gx")
    for k, place in enumerate(peers):
        start = pl.multiple_of(peer(member, len(PEERS), place, sign) * span, span)
        target_ref[k * span : (k + 1) * span] = source_ref[pl.ds(start, span), :]


def forward_body(peers, x_any, by_any, bz_any, *refs):
    outs, refs = refs[: len(peers)], refs[len(peers) :]
    x_ref, by_ref, bz_ref, turn_ref, rows_ref, by3_ref, bz3_ref, x_sem, b_sem = refs
    total, rows, y, z = x_ref.shape
    size = outs[0].shape[1]
    span = size // rows
    tables = [
        pltpu.make_async_copy(source, target, b_sem.at[k])
        for k, (source, target) in enumerate(((by_any, by_ref), (bz_any, bz_ref)))
    ]
    planes = [pltpu.make_async_copy(x_any.at[t], x_ref.at[t], x_sem.at[t]) for t in range(total)]
    for copy in planes + tables:
        copy.start()
    for copy in planes + tables:
        copy.wait()
    turn_ref[...] = by_ref[...].T
    gather_rows(turn_ref, rows_ref, peers, 1)
    by3_ref[...] = left3(rows_ref[...])
    bz3_ref[...] = right3(bz_ref[...])

    vol = [mm(left3(x_ref[t].reshape(rows * y, z)), bz3_ref[...]) for t in range(total)]
    for first in range(0, total, 4):
        times = range(first, first + 4)
        for a in range(rows):
            plane = jnp.concatenate([vol[t][a * y : (a + 1) * y] for t in times], axis=1)
            plane = mm(by3_ref[...], right3(plane))
            for k, out in enumerate(outs):
                for i, t in enumerate(times):
                    out[t, pl.ds(a, span, stride=rows), :] = plane[
                        k * span : (k + 1) * span, i * z : (i + 1) * z
                    ]


def forward_yz(x, by, bz, peers):
    t, a, y, z = x.shape
    span = y // len(PEERS)
    return pl.pallas_call(
        partial(forward_body, peers),
        in_specs=[ANY] * 3,
        out_specs=[VMEM] * len(peers),
        out_shape=[array(t, a * span, z)] * len(peers),
        scratch_shapes=[
            pltpu.VMEM(x.shape, f32),
            pltpu.VMEM((y, y), f32),
            pltpu.VMEM((z, z), f32),
            pltpu.VMEM((y, y), f32),
            pltpu.VMEM((len(peers) * span, y), f32),
            pltpu.VMEM((len(peers) * span, 3 * y), bf16),
            pltpu.VMEM((3 * z, z), bf16),
            pltpu.SemaphoreType.DMA((t,)),
            pltpu.SemaphoreType.DMA((2,)),
        ],
        compiler_params=params(),
        cost_estimate=cost(6 * t * a * len(peers) * span * z * (y + z), 8 * t * a * y * z),
        name="forward_yz",
    )(x, by, bz)


def backward_planes(times, rows, by3_ref, bz3_ref, pieces, mid_ref):
    size, z = pieces[0].shape[1:]
    span = size // rows
    for t in times:
        flat = jnp.concatenate([piece[t] for piece in pieces], axis=0)
        mid_ref[t] = mm(left3(flat), bz3_ref[...])
    for a in range(rows):
        plane = [
            jnp.concatenate(
                [mid_ref[t, pl.ds(k * size + a, span, stride=rows), :] for k in range(len(pieces))],
                axis=0,
            )
            for t in times
        ]
        plane = mm(by3_ref[...], right3(jnp.concatenate(plane, axis=1)))
        for i, t in enumerate(times):
            yield t, a, plane[:, i * z : (i + 1) * z]


def backward_early_body(by3_ref, bz3_ref, *refs):
    pieces, (out_ref, mid_ref) = refs[:-2], refs[-2:]
    total, rows = out_ref.shape[:2]
    for first in range(0, total, 2):
        times = (first, first + 1)
        for t, a, plane in backward_planes(times, rows, by3_ref, bz3_ref, pieces, mid_ref):
            out_ref[t, a] = plane


def backward_late_body(by3_ref, bz3_ref, early_ref, *refs):
    pieces, (out_any, out_ref, mid_ref, sem) = refs[:-4], refs[-4:]
    total, rows = out_ref.shape[:2]
    copies = []
    for first in range(0, total, 2):
        times = (first, first + 1)
        for t, a, plane in backward_planes(times, rows, by3_ref, bz3_ref, pieces, mid_ref):
            out_ref[t, a] = early_ref[t, a] + plane
        if first == 0:
            continue
        for t in range(0 if first == 2 else first, first + 2):
            copies.append(pltpu.make_async_copy(out_ref.at[t], out_any.at[t], sem.at[t]))
            copies[-1].start()
    for copy in copies:
        copy.wait()


def backward_yz(pieces, by3, bz3, early=()):
    y, z = by3.shape[0], bz3.shape[1]
    t, size = pieces[0].shape[:2]
    a = size * len(PEERS) // y
    mid = pltpu.VMEM((t, len(pieces) * size, z), f32)
    scratch = [pltpu.VMEM((t, a, y, z), f32), mid, pltpu.SemaphoreType.DMA((t,))]
    return pl.pallas_call(
        backward_late_body if early else backward_early_body,
        in_specs=[VMEM] * (2 + len(early) + len(pieces)),
        out_specs=ANY if early else VMEM,
        out_shape=array(t, a, y, z),
        scratch_shapes=scratch if early else [mid],
        compiler_params=params(),
        cost_estimate=cost(6 * t * size * len(pieces) * z * (y + z), 8 * t * a * y * z),
        name="backward_yz",
    )(by3, bz3, *early, *pieces)


def length(steps_ref, at):
    total = steps_ref.shape[0]
    here = steps_ref[jnp.minimum(at, total - 1)] / total
    return jnp.where(at < total, here, 0.0)


def row_terms(eigen, steps_ref, at):
    now, then = length(steps_ref, at), length(steps_ref, at + 1)
    closing = jnp.where(at == steps_ref.shape[0] - 1, 0.5, 0.0)
    main = eigen * ((now + then) / 3.0) + closing
    sub = eigen * (now / 6.0) - 0.5
    sup = eigen * (then / 6.0) + 0.5
    return main, sub, sup


def mode_sums(ex_ref, ey_ref, ez_ref, j):
    x, z = ex_ref.shape[1], ez_ref.shape[1]
    along_x = jnp.broadcast_to(ex_ref[...], (z, x)).T
    return (along_x + ey_ref[j]) + ez_ref[...]


def prepare_body(steps_ref, ex_ref, ey_ref, ez_ref, bx_ref, by_ref, bz_ref, *refs):
    inv_ref, mul_ref, ratio_ref, v_ref, w_ref, bx3_ref, *more, bz3_ref = refs[:11]
    bx3_back_refs, by3_refs = more[:2], more[2:]
    sums_ref, turn_ref, rows_ref = refs[11:]
    half = rows_ref.shape[0] // 2
    total, modes, lanes = inv_ref.shape
    x, members = ex_ref.shape[1], len(PEERS)
    gather_rows(bx_ref, rows_ref, PEERS, -1)
    bx3_ref[...] = left3(rows_ref[...].T)
    for peers, ref in zip((FAR, NEAR), bx3_back_refs):
        gather_rows(bx_ref, rows_ref.at[:half], peers, 1)
        ref[...] = left3(rows_ref[:half])
    turn_ref[...] = by_ref[...].T
    gather_rows(turn_ref, rows_ref, PEERS, -1)
    for k, ref in enumerate(by3_refs):
        ref[...] = left3(rows_ref[k * half : (k + 1) * half].T)
    bz3_ref[...] = right3(bz_ref[...].T)

    span = ey_ref.shape[0] // members
    member = lax.axis_index("gx")
    for j in range(span):
        sums_ref[j * x : (j + 1) * x] = mode_sums(ex_ref, ey_ref, ez_ref, member * span + j)
    begin = lax.axis_index("ta") * total
    size = 32

    def block(n, carry):
        mine = pl.ds(pl.multiple_of(n * size, size), size)
        eigen = sums_ref[mine, :]
        ratios, fronts = [], []
        for k in range(total):
            main, sub, sup = row_terms(eigen, steps_ref, begin + k)
            inverse = 1.0 / (main - sub * ratios[-1] if k else main)
            factor = sub * inverse
            ratios.append(sup * inverse)
            fronts.append(-factor * fronts[-1] if k else factor)
            inv_ref[k, mine, :] = inverse
            mul_ref[k, mine, :] = factor
            ratio_ref[k, mine, :] = ratios[-1]
        low, last = fronts[-1], ratios[-1]
        v_ref[total - 1, mine, :] = low
        w_ref[total - 1, mine, :] = last
        for k in reversed(range(total - 1)):
            low = fronts[k] - ratios[k] * low
            last = -ratios[k] * last
            v_ref[k, mine, :] = low
            w_ref[k, mine, :] = last
        return carry

    lax.fori_loop(0, modes // size, block, 0)


def prepare(steps, sums, bx, by, bz, rows):
    x, y, z = bx.shape[0], by.shape[0], bz.shape[0]
    modes = x * y // len(PEERS)
    table = lambda *shape: jax.ShapeDtypeStruct(shape, bf16)
    return pl.pallas_call(
        prepare_body,
        in_specs=[SMEM, VMEM, SMEM, VMEM, VMEM, VMEM, VMEM],
        out_specs=[VMEM] * 11,
        out_shape=[array(rows, modes, z)] * 5
        + [table(x, 3 * x)]
        + [table(x // 2, 3 * x)] * 2
        + [table(y, 3 * y // 2)] * 2
        + [table(3 * z, z)],
        scratch_shapes=[
            pltpu.VMEM((modes, z), f32),
            pltpu.VMEM((y, y), f32),
            pltpu.VMEM((x, x), f32),
        ],
        compiler_params=params(),
        cost_estimate=cost(30 * rows * modes * z, 20 * rows * modes * z),
        name="prepare",
    )(steps, *sums, bx, by, bz)


def reduced_body(rows, steps_ref, ex_ref, ey_ref, ez_ref, cl_ref, e_ref, a_ref, k_ref, b_ref, q_ref, sums_ref):
    count, share = cl_ref.shape[:2]
    x, span = ex_ref.shape[1], ey_ref.shape[0] // len(PEERS)
    first = lax.axis_index("ta") * share
    sums_ref[...] = mode_sums(ex_ref, ey_ref, ez_ref, lax.axis_index("gx") * span + first // x)
    eigen = sums_ref[pl.ds(pl.multiple_of(lax.rem(first, x), share), share), :]

    def block(j, carry):
        inverses, subs, ratios = [], [], []
        for k in range(rows):
            main, sub, sup = row_terms(eigen, steps_ref, j * rows + k)
            inverse = 1.0 / (main - sub * ratios[-1] if k else main)
            inverses.append(inverse)
            subs.append(sub)
            ratios.append(sup * inverse)
        front = subs[0] * inverses[0]
        fronts = [front]
        for k in range(1, rows):
            front = -(subs[k] * inverses[k]) * front
            fronts.append(front)
        last = ratios[rows - 1]
        low = fronts[rows - 1]
        cl_ref[j] = low
        e_ref[j] = last
        for k in reversed(range(rows - 1)):
            low = fronts[k] - ratios[k] * low
            last = -ratios[k] * last
        a_ref[j] = low
        b_ref[j] = last
        return carry

    lax.fori_loop(0, count, block, 0, unroll=4)

    def sweep(j, q_before):
        v_last, w_last, v_first, w_first = cl_ref[j], e_ref[j], a_ref[j], b_ref[j]
        scale = 1.0 / (1.0 - v_first * q_before)
        back = w_first * scale
        q_now = w_last + v_last * q_before * back
        e_now = v_last * scale
        cl_ref[j] = e_now * q_before
        e_ref[j] = e_now
        a_ref[j] = scale
        k_ref[j] = v_first * scale
        b_ref[j] = back
        q_ref[j] = q_now
        return q_now

    lax.fori_loop(0, count, sweep, jnp.zeros_like(eigen))


def reduced_terms(steps, sums, count, rows, share):
    x, z = sums[0].shape[1], sums[2].shape[1]
    return pl.pallas_call(
        partial(reduced_body, rows),
        in_specs=[SMEM, VMEM, SMEM, VMEM],
        out_specs=[VMEM] * 6,
        out_shape=[array(count, share, z)] * 6,
        scratch_shapes=[pltpu.VMEM((x, z), f32)],
        compiler_params=params(),
        cost_estimate=cost(40 * rows * count * share * z, 24 * count * share * z),
        name="reduced_terms",
    )(steps, *sums)


def interface_body(g_ref, cl_ref, e_ref, a_ref, k_ref, b_ref, q_ref, out_ref, fh_ref):
    count = g_ref.shape[0]
    zero = jnp.zeros(g_ref.shape[2:], f32)

    def down(j, before):
        first, last = g_ref[j, 0], g_ref[j, 1]
        out_ref[j, 0] = before
        fh_ref[j] = a_ref[j] * first - k_ref[j] * before
        return (last + cl_ref[j] * first) - e_ref[j] * before

    lax.fori_loop(0, count, down, zero, unroll=8)

    def up(i, after):
        j = count - 1 - i
        out_ref[j, 1] = after

        @pl.when(j < count - 1)
        def _():
            out_ref[j + 1, 0] = out_ref[j + 1, 0] - q_ref[j] * after

        return fh_ref[j] - b_ref[j] * after

    lax.fori_loop(0, count, up, zero, unroll=8)


def interface_solve(g, terms):
    return pl.pallas_call(
        interface_body,
        in_specs=[VMEM] * 7,
        out_specs=VMEM,
        out_shape=array(*g.shape),
        scratch_shapes=[pltpu.VMEM(g.shape[:1] + g.shape[2:], f32)],
        compiler_params=params(),
        cost_estimate=cost(6 * g.size, 20 * g.size),
        name="interface_solve",
    )(g, *terms)


def transform_pair(table, planes):
    lanes = planes[0].shape[1]
    both = mm(table, right3(jnp.concatenate(planes, axis=1)))
    return both[:, :lanes], both[:, lanes:]


def eliminate_body(bx3_ref, inv_ref, mul_ref, ratio_ref, *refs):
    pieces, (g_ref, ends_ref) = refs[:-2], refs[-2:]
    total, modes, lanes = g_ref.shape
    x = bx3_ref.shape[0]
    span = x // len(pieces)
    for t in range(0, total, 2):
        for j in range(modes // x):
            mine = slice(j * x, (j + 1) * x)
            spectral = transform_pair(
                bx3_ref[...],
                [
                    jnp.concatenate([piece[k, j * span : (j + 1) * span, :] for piece in pieces], axis=0)
                    for k in (t, t + 1)
                ],
            )
            for k, values in zip((t, t + 1), spectral):
                values = values * inv_ref[k, mine]
                g_ref[k, mine] = values - mul_ref[k, mine] * g_ref[k - 1, mine] if k else values

    split_shape = (ends_ref.shape[0], modes // ends_ref.shape[0], lanes)
    now = g_ref[total - 1]
    ends_ref[:, 1] = now.reshape(split_shape)
    for k in reversed(range(total - 1)):
        now = g_ref[k] - ratio_ref[k] * now
        g_ref[k] = now
    ends_ref[:, 0] = now.reshape(split_shape)


def eliminate(pieces, bx3, factors, count):
    t, rows, z = pieces[0].shape
    x = bx3.shape[0]
    modes = rows * len(pieces)
    return pl.pallas_call(
        eliminate_body,
        in_specs=[VMEM] * (4 + len(pieces)),
        out_specs=[VMEM] * 2,
        out_shape=[array(t, modes, z), array(count, 2, modes // count, z)],
        compiler_params=params(),
        cost_estimate=cost(6 * t * modes * x * z, 20 * t * modes * z),
        name="eliminate",
    )(bx3, *factors, *pieces)


def return_body(bx3_ref, v_ref, w_ref, g_ref, ends_ref, *outs):
    total, modes, lanes = g_ref.shape
    span = bx3_ref.shape[0] // len(outs)
    x = bx3_ref.shape[1] // 3
    share = modes // ends_ref.shape[0]
    for j in range(modes // x):
        mine = slice(j * x, (j + 1) * x)
        owners = slice(j * x // share, (j + 1) * x // share)
        before = ends_ref[owners, 0].reshape(x, lanes)
        after = ends_ref[owners, 1].reshape(x, lanes)
        for t in range(0, total, 2):
            cells = transform_pair(
                bx3_ref[...],
                [
                    g_ref[k, mine] - v_ref[k, mine] * before - w_ref[k, mine] * after
                    for k in (t, t + 1)
                ],
            )
            for k, cell in zip((t, t + 1), cells):
                for i, out in enumerate(outs):
                    out[k, j * span : (j + 1) * span, :] = cell[i * span : (i + 1) * span]


def return_x(g, ends, bx3, v, w):
    t, modes, z = g.shape
    x, pieces = bx3.shape[1] // 3, len(PEERS) * 3 * bx3.shape[0] // bx3.shape[1]
    return pl.pallas_call(
        return_body,
        in_specs=[VMEM] * 5,
        out_specs=[VMEM] * pieces,
        out_shape=[array(t, modes // len(PEERS), z)] * pieces,
        compiler_params=params(),
        cost_estimate=cost(6 * t * modes * bx3.shape[0] * z, 16 * t * modes * z),
        name="return_x",
    )(bx3, v, w, g, ends)


def local(right_side, basis_x, basis_y, basis_z, eig_x, eig_y, eig_z, steps):
    rows = right_side.shape[0]
    count = lax.axis_size("ta")
    sums = (eig_x[None, :], eig_y, eig_z[None, :])
    share = basis_x.shape[0] * basis_y.shape[0] // (lax.axis_size("gx") * count)
    hbm = lambda value: pltpu.with_memory_space_constraint(value, pltpu.HBM)

    given = (hbm(right_side), hbm(basis_y), hbm(basis_z))
    sent = forward_yz(*given, FAR)
    rest = forward_yz(*given, NEAR)
    moved = exchange([rest[0], *sent, *rest[1:]])
    terms = list(reduced_terms(steps, sums, count, rows, share))
    *factors, v, w, bx3, bx3_far, bx3_near, by3_early, by3_late, bz3 = prepare(steps, sums, basis_x, basis_y, basis_z, rows)
    moved[0], terms[0], bx3 = lax.optimization_barrier((moved[0], terms[0], bx3))
    g, ends = eliminate(moved, bx3, factors, count)
    ends = lax.all_to_all(ends, "ta", 0, 0, tiled=True)
    ends = interface_solve(ends, terms)
    ends = lax.all_to_all(ends, "ta", 0, 0, tiled=True)
    sent = return_x(g, ends, bx3_far, v, w)
    rest = return_x(g, ends, bx3_near, v, w)
    moved = exchange([rest[0], *sent, *rest[1:]])
    early = backward_yz(moved[:4], by3_early, bz3)
    return backward_yz(moved[4:], by3_late, bz3, (early,))


def solution(mesh):
    return jax.shard_map(
        local,
        mesh=mesh,
        in_specs=(P("ta", "gx", None, None), P(), P(), P(), P(), P(), P(), P()),
        out_specs=P("ta", "gx", None, None),
        check_vma=False,
    )
```

```python
from functools import partial

import jax
import jax.numpy as jnp
from jax import lax
from jax.experimental import pallas as pl
from jax.experimental.pallas import tpu as pltpu
from jax.sharding import PartitionSpec as P

f32, bf16 = jnp.float32, jnp.bfloat16
params = partial(pltpu.CompilerParams, vmem_limit_bytes=12 * 2**20)
VMEM = pl.BlockSpec(memory_space=pltpu.VMEM)
SMEM = pl.BlockSpec(memory_space=pltpu.SMEM)
ANY = pl.BlockSpec(memory_space=pl.ANY)

PEERS = ((0, 0), (2, 0), (2, 1), (1, 0), (3, 0), (1, 1), (3, 1), (0, 1))


def peer(member, members, place, sign):
    chips, core = place
    ring = members // 2
    far = lax.rem(member // 2 + (sign * chips) % ring, ring)
    own = lax.rem(member, 2)
    return far * 2 + (1 - own if core else own)


def send(piece, place, members):
    chips, core = place
    pairs = [(i, ((i // 2 + chips) * 2 + (i % 2 + core) % 2) % members) for i in range(members)]
    return lax.ppermute(piece, "gx", pairs)


def exchange(pieces):
    moved = [send(piece, place, len(PEERS)) for piece, place in zip(pieces[1:], PEERS[1:])]
    return [pieces[0]] + moved


def split(x):
    high = x.astype(bf16)
    return high, (x - high.astype(f32)).astype(bf16)


def left3(x):
    high, low = split(x)
    return jnp.concatenate([high, high, low], axis=1)


def right3(x):
    high, low = split(x)
    return jnp.concatenate([high, low, high], axis=0)


mm = partial(jnp.dot, preferred_element_type=f32)


def cost(flops, bytes_accessed):
    return pl.CostEstimate(flops=int(flops), bytes_accessed=int(bytes_accessed), transcendentals=0)


def array(*shape):
    return jax.ShapeDtypeStruct(shape, f32)


def gather_rows(source_ref, target_ref, peers, sign):
    span = target_ref.shape[0] // len(peers)
    member = lax.axis_index("gx")
    for k, place in enumerate(peers):
        start = pl.multiple_of(peer(member, len(PEERS), place, sign) * span, span)
        target_ref[k * span : (k + 1) * span] = source_ref[pl.ds(start, span), :]


def forward_body(peers, x_any, by_any, bz_any, *refs):
    outs, refs = refs[: len(peers)], refs[len(peers) :]
    x_ref, by_ref, bz_ref, turn_ref, rows_ref, by3_ref, bz3_ref, x_sem, b_sem = refs
    total, rows, y, z = x_ref.shape
    size = outs[0].shape[1]
    span = size // rows
    tables = [
        pltpu.make_async_copy(source, target, b_sem.at[k])
        for k, (source, target) in enumerate(((by_any, by_ref), (bz_any, bz_ref)))
    ]
    planes = [pltpu.make_async_copy(x_any.at[t], x_ref.at[t], x_sem.at[t]) for t in range(total)]
    for copy in planes + tables:
        copy.start()
    for copy in planes + tables:
        copy.wait()
    turn_ref[...] = by_ref[...].T
    gather_rows(turn_ref, rows_ref, peers, 1)
    by3_ref[...] = left3(rows_ref[...])
    bz3_ref[...] = right3(bz_ref[...])

    vol = [mm(left3(x_ref[t].reshape(rows * y, z)), bz3_ref[...]) for t in range(total)]
    for first in range(0, total, 4):
        times = range(first, first + 4)
        for a in range(rows):
            plane = jnp.concatenate([vol[t][a * y : (a + 1) * y] for t in times], axis=1)
            plane = mm(by3_ref[...], right3(plane))
            for k, out in enumerate(outs):
                for i, t in enumerate(times):
                    out[t, pl.ds(a, span, stride=rows), :] = plane[
                        k * span : (k + 1) * span, i * z : (i + 1) * z
                    ]


def forward_yz(x, by, bz, peers):
    t, a, y, z = x.shape
    span = y // len(PEERS)
    return pl.pallas_call(
        partial(forward_body, peers),
        in_specs=[ANY] * 3,
        out_specs=[VMEM] * len(peers),
        out_shape=[array(t, a * span, z)] * len(peers),
        scratch_shapes=[
            pltpu.VMEM(x.shape, f32),
            pltpu.VMEM((y, y), f32),
            pltpu.VMEM((z, z), f32),
            pltpu.VMEM((y, y), f32),
            pltpu.VMEM((len(peers) * span, y), f32),
            pltpu.VMEM((len(peers) * span, 3 * y), bf16),
            pltpu.VMEM((3 * z, z), bf16),
            pltpu.SemaphoreType.DMA((t,)),
            pltpu.SemaphoreType.DMA((2,)),
        ],
        compiler_params=params(),
        cost_estimate=cost(6 * t * a * len(peers) * span * z * (y + z), 8 * t * a * y * z),
        name="forward_yz",
    )(x, by, bz)


def backward_planes(times, rows, by3_ref, bz3_ref, pieces, mid_ref):
    size, z = pieces[0].shape[1:]
    span = size // rows
    for t in times:
        flat = jnp.concatenate([piece[t] for piece in pieces], axis=0)
        mid_ref[t] = mm(left3(flat), bz3_ref[...])
    for a in range(rows):
        plane = [
            jnp.concatenate(
                [mid_ref[t, pl.ds(k * size + a, span, stride=rows), :] for k in range(len(pieces))],
                axis=0,
            )
            for t in times
        ]
        plane = mm(by3_ref[...], right3(jnp.concatenate(plane, axis=1)))
        for i, t in enumerate(times):
            yield t, a, plane[:, i * z : (i + 1) * z]


def backward_early_body(by3_ref, bz3_ref, *refs):
    pieces, (out_ref, mid_ref) = refs[:-2], refs[-2:]
    total, rows = out_ref.shape[:2]
    for first in range(0, total, 2):
        times = (first, first + 1)
        for t, a, plane in backward_planes(times, rows, by3_ref, bz3_ref, pieces, mid_ref):
            out_ref[t, a] = plane


def backward_late_body(by3_ref, bz3_ref, early_ref, *refs):
    pieces, (out_any, out_ref, mid_ref, sem) = refs[:-4], refs[-4:]
    total, rows = out_ref.shape[:2]
    copies = []
    for first in range(0, total, 2):
        times = (first, first + 1)
        for t, a, plane in backward_planes(times, rows, by3_ref, bz3_ref, pieces, mid_ref):
            out_ref[t, a] = early_ref[t, a] + plane
        for t in times:
            copies.append(pltpu.make_async_copy(out_ref.at[t], out_any.at[t], sem.at[t]))
            copies[-1].start()
    for copy in copies:
        copy.wait()


def backward_yz(pieces, by3, bz3, early=()):
    y, z = by3.shape[0], bz3.shape[1]
    t, size = pieces[0].shape[:2]
    a = size * len(PEERS) // y
    mid = pltpu.VMEM((t, len(pieces) * size, z), f32)
    scratch = [pltpu.VMEM((t, a, y, z), f32), mid, pltpu.SemaphoreType.DMA((t,))]
    return pl.pallas_call(
        backward_late_body if early else backward_early_body,
        in_specs=[VMEM] * (2 + len(early) + len(pieces)),
        out_specs=ANY if early else VMEM,
        out_shape=array(t, a, y, z),
        scratch_shapes=scratch if early else [mid],
        compiler_params=params(),
        cost_estimate=cost(6 * t * size * len(pieces) * z * (y + z), 8 * t * a * y * z),
        name="backward_yz",
    )(by3, bz3, *early, *pieces)


def length(steps_ref, at):
    total = steps_ref.shape[0]
    here = steps_ref[jnp.minimum(at, total - 1)] / total
    return jnp.where(at < total, here, 0.0)


def row_terms(eigen, steps_ref, at):
    now, then = length(steps_ref, at), length(steps_ref, at + 1)
    closing = jnp.where(at == steps_ref.shape[0] - 1, 0.5, 0.0)
    main = eigen * ((now + then) / 3.0) + closing
    sub = eigen * (now / 6.0) - 0.5
    sup = eigen * (then / 6.0) + 0.5
    return main, sub, sup


def mode_sums(ex_ref, ey_ref, ez_ref, j):
    x, z = ex_ref.shape[1], ez_ref.shape[1]
    along_x = jnp.broadcast_to(ex_ref[...], (z, x)).T
    return (along_x + ey_ref[j]) + ez_ref[...]


def prepare_body(steps_ref, ex_ref, ey_ref, ez_ref, bx_ref, by_ref, bz_ref, *refs):
    inv_ref, mul_ref, ratio_ref, v_ref, w_ref, bx3_ref, bx3_back_ref, *by3_refs, bz3_ref = refs[:10]
    sums_ref, turn_ref, rows_ref = refs[10:]
    total, modes, lanes = inv_ref.shape
    x, members = ex_ref.shape[1], len(PEERS)
    gather_rows(bx_ref, rows_ref, PEERS, -1)
    bx3_ref[...] = left3(rows_ref[...].T)
    gather_rows(bx_ref, rows_ref, PEERS, 1)
    bx3_back_ref[...] = left3(rows_ref[...])
    turn_ref[...] = by_ref[...].T
    gather_rows(turn_ref, rows_ref, PEERS, -1)
    half = rows_ref.shape[0] // 2
    for k, ref in enumerate(by3_refs):
        ref[...] = left3(rows_ref[k * half : (k + 1) * half].T)
    bz3_ref[...] = right3(bz_ref[...].T)

    span = ey_ref.shape[0] // members
    member = lax.axis_index("gx")
    for j in range(span):
        sums_ref[j * x : (j + 1) * x] = mode_sums(ex_ref, ey_ref, ez_ref, member * span + j)
    begin = lax.axis_index("ta") * total
    size = 32

    def block(n, carry):
        mine = pl.ds(pl.multiple_of(n * size, size), size)
        eigen = sums_ref[mine, :]
        ratios, fronts = [], []
        for k in range(total):
            main, sub, sup = row_terms(eigen, steps_ref, begin + k)
            inverse = 1.0 / (main - sub * ratios[-1] if k else main)
            factor = sub * inverse
            ratios.append(sup * inverse)
            fronts.append(-factor * fronts[-1] if k else factor)
            inv_ref[k, mine, :] = inverse
            mul_ref[k, mine, :] = factor
            ratio_ref[k, mine, :] = ratios[-1]
        low, last = fronts[-1], ratios[-1]
        v_ref[total - 1, mine, :] = low
        w_ref[total - 1, mine, :] = last
        for k in reversed(range(total - 1)):
            low = fronts[k] - ratios[k] * low
            last = -ratios[k] * last
            v_ref[k, mine, :] = low
            w_ref[k, mine, :] = last
        return carry

    lax.fori_loop(0, modes // size, block, 0)


def prepare(steps, sums, bx, by, bz, rows):
    x, y, z = bx.shape[0], by.shape[0], bz.shape[0]
    modes = x * y // len(PEERS)
    table = lambda *shape: jax.ShapeDtypeStruct(shape, bf16)
    return pl.pallas_call(
        prepare_body,
        in_specs=[SMEM, VMEM, SMEM, VMEM, VMEM, VMEM, VMEM],
        out_specs=[VMEM] * 10,
        out_shape=[array(rows, modes, z)] * 5
        + [table(x, 3 * x)] * 2
        + [table(y, 3 * y // 2)] * 2
        + [table(3 * z, z)],
        scratch_shapes=[
            pltpu.VMEM((modes, z), f32),
            pltpu.VMEM((y, y), f32),
            pltpu.VMEM((x, x), f32),
        ],
        compiler_params=params(),
        cost_estimate=cost(30 * rows * modes * z, 20 * rows * modes * z),
        name="prepare",
    )(steps, *sums, bx, by, bz)


def reduced_body(rows, steps_ref, ex_ref, ey_ref, ez_ref, cl_ref, e_ref, a_ref, k_ref, b_ref, q_ref, sums_ref):
    count, share = cl_ref.shape[:2]
    x, span = ex_ref.shape[1], ey_ref.shape[0] // len(PEERS)
    first = lax.axis_index("ta") * share
    sums_ref[...] = mode_sums(ex_ref, ey_ref, ez_ref, lax.axis_index("gx") * span + first // x)
    eigen = sums_ref[pl.ds(pl.multiple_of(lax.rem(first, x), share), share), :]

    def block(j, carry):
        inverses, subs, ratios = [], [], []
        for k in range(rows):
            main, sub, sup = row_terms(eigen, steps_ref, j * rows + k)
            inverse = 1.0 / (main - sub * ratios[-1] if k else main)
            inverses.append(inverse)
            subs.append(sub)
            ratios.append(sup * inverse)
        front = subs[0] * inverses[0]
        fronts = [front]
        for k in range(1, rows):
            front = -(subs[k] * inverses[k]) * front
            fronts.append(front)
        last = ratios[rows - 1]
        low = fronts[rows - 1]
        cl_ref[j] = low
        e_ref[j] = last
        for k in reversed(range(rows - 1)):
            low = fronts[k] - ratios[k] * low
            last = -ratios[k] * last
        a_ref[j] = low
        b_ref[j] = last
        return carry

    lax.fori_loop(0, count, block, 0, unroll=4)

    def sweep(j, q_before):
        v_last, w_last, v_first, w_first = cl_ref[j], e_ref[j], a_ref[j], b_ref[j]
        scale = 1.0 / (1.0 - v_first * q_before)
        back = w_first * scale
        q_now = w_last + v_last * q_before * back
        e_now = v_last * scale
        cl_ref[j] = e_now * q_before
        e_ref[j] = e_now
        a_ref[j] = scale
        k_ref[j] = v_first * scale
        b_ref[j] = back
        q_ref[j] = q_now
        return q_now

    lax.fori_loop(0, count, sweep, jnp.zeros_like(eigen))


def reduced_terms(steps, sums, count, rows, share):
    x, z = sums[0].shape[1], sums[2].shape[1]
    return pl.pallas_call(
        partial(reduced_body, rows),
        in_specs=[SMEM, VMEM, SMEM, VMEM],
        out_specs=[VMEM] * 6,
        out_shape=[array(count, share, z)] * 6,
        scratch_shapes=[pltpu.VMEM((x, z), f32)],
        compiler_params=params(),
        cost_estimate=cost(40 * rows * count * share * z, 24 * count * share * z),
        name="reduced_terms",
    )(steps, *sums)


def interface_body(g_ref, cl_ref, e_ref, a_ref, k_ref, b_ref, q_ref, out_ref, fh_ref):
    count = g_ref.shape[0]
    zero = jnp.zeros(g_ref.shape[2:], f32)

    def down(j, before):
        first, last = g_ref[j, 0], g_ref[j, 1]
        out_ref[j, 0] = before
        fh_ref[j] = a_ref[j] * first - k_ref[j] * before
        return (last + cl_ref[j] * first) - e_ref[j] * before

    lax.fori_loop(0, count, down, zero, unroll=32)

    def up(i, after):
        j = count - 1 - i
        out_ref[j, 1] = after

        @pl.when(j < count - 1)
        def _():
            out_ref[j + 1, 0] = out_ref[j + 1, 0] - q_ref[j] * after

        return fh_ref[j] - b_ref[j] * after

    lax.fori_loop(0, count, up, zero, unroll=32)


def interface_solve(g, terms):
    return pl.pallas_call(
        interface_body,
        in_specs=[VMEM] * 7,
        out_specs=VMEM,
        out_shape=array(*g.shape),
        scratch_shapes=[pltpu.VMEM(g.shape[:1] + g.shape[2:], f32)],
        compiler_params=params(),
        cost_estimate=cost(6 * g.size, 20 * g.size),
        name="interface_solve",
    )(g, *terms)


def transform_pair(table, planes):
    lanes = planes[0].shape[1]
    both = mm(table, right3(jnp.concatenate(planes, axis=1)))
    return both[:, :lanes], both[:, lanes:]


def eliminate_body(bx3_ref, inv_ref, mul_ref, ratio_ref, *refs):
    pieces, (g_ref, ends_ref) = refs[:-2], refs[-2:]
    total, modes, lanes = g_ref.shape
    x = bx3_ref.shape[0]
    span = x // len(pieces)
    for t in range(0, total, 2):
        for j in range(modes // x):
            mine = slice(j * x, (j + 1) * x)
            spectral = transform_pair(
                bx3_ref[...],
                [
                    jnp.concatenate([piece[k, j * span : (j + 1) * span, :] for piece in pieces], axis=0)
                    for k in (t, t + 1)
                ],
            )
            for k, values in zip((t, t + 1), spectral):
                values = values * inv_ref[k, mine]
                g_ref[k, mine] = values - mul_ref[k, mine] * g_ref[k - 1, mine] if k else values

    split_shape = (ends_ref.shape[0], modes // ends_ref.shape[0], lanes)
    now = g_ref[total - 1]
    ends_ref[:, 1] = now.reshape(split_shape)
    for k in reversed(range(total - 1)):
        now = g_ref[k] - ratio_ref[k] * now
        g_ref[k] = now
    ends_ref[:, 0] = now.reshape(split_shape)


def eliminate(pieces, bx3, factors, count):
    t, rows, z = pieces[0].shape
    x = bx3.shape[0]
    modes = rows * len(pieces)
    return pl.pallas_call(
        eliminate_body,
        in_specs=[VMEM] * (4 + len(pieces)),
        out_specs=[VMEM] * 2,
        out_shape=[array(t, modes, z), array(count, 2, modes // count, z)],
        compiler_params=params(),
        cost_estimate=cost(6 * t * modes * x * z, 20 * t * modes * z),
        name="eliminate",
    )(bx3, *factors, *pieces)


def return_body(bx3_ref, v_ref, w_ref, g_ref, ends_ref, *outs):
    total, modes, lanes = g_ref.shape
    x = bx3_ref.shape[0]
    span = x // len(outs)
    share = modes // ends_ref.shape[0]
    for j in range(modes // x):
        mine = slice(j * x, (j + 1) * x)
        owners = slice(j * x // share, (j + 1) * x // share)
        before = ends_ref[owners, 0].reshape(x, lanes)
        after = ends_ref[owners, 1].reshape(x, lanes)
        for t in range(0, total, 2):
            cells = transform_pair(
                bx3_ref[...],
                [
                    g_ref[k, mine] - v_ref[k, mine] * before - w_ref[k, mine] * after
                    for k in (t, t + 1)
                ],
            )
            for k, cell in zip((t, t + 1), cells):
                for i, out in enumerate(outs):
                    out[k, j * span : (j + 1) * span, :] = cell[i * span : (i + 1) * span]


def return_x(g, ends, bx3, v, w):
    t, modes, z = g.shape
    x, members = bx3.shape[0], len(PEERS)
    return pl.pallas_call(
        return_body,
        in_specs=[VMEM] * 5,
        out_specs=[VMEM] * members,
        out_shape=[array(t, modes // members, z)] * members,
        compiler_params=params(),
        cost_estimate=cost(6 * t * modes * x * z, 16 * t * modes * z),
        name="return_x",
    )(bx3, v, w, g, ends)


def local(right_side, basis_x, basis_y, basis_z, eig_x, eig_y, eig_z, steps):
    rows = right_side.shape[0]
    count = lax.axis_size("ta")
    sums = (eig_x[None, :], eig_y, eig_z[None, :])
    share = basis_x.shape[0] * basis_y.shape[0] // (lax.axis_size("gx") * count)
    hbm = lambda value: pltpu.with_memory_space_constraint(value, pltpu.HBM)

    given = (hbm(right_side), hbm(basis_y), hbm(basis_z))
    far, near = PEERS[1:5], PEERS[:1] + PEERS[5:]
    sent = forward_yz(*given, far)
    rest = forward_yz(*given, near)
    moved = exchange([rest[0], *sent, *rest[1:]])
    terms = list(reduced_terms(steps, sums, count, rows, share))
    *factors, v, w, bx3, bx3_back, by3_early, by3_late, bz3 = prepare(steps, sums, basis_x, basis_y, basis_z, rows)
    moved[0], terms[0], bx3 = lax.optimization_barrier((moved[0], terms[0], bx3))
    g, ends = eliminate(moved, bx3, factors, count)
    ends = lax.all_to_all(ends, "ta", 0, 0, tiled=True)
    ends = interface_solve(ends, terms)
    ends = lax.all_to_all(ends, "ta", 0, 0, tiled=True)
    moved = exchange(return_x(g, ends, bx3_back, v, w))
    early = backward_yz(moved[:4], by3_early, bz3)
    return backward_yz(moved[4:], by3_late, bz3, (early,))


def solution(mesh):
    return jax.shard_map(
        local,
        mesh=mesh,
        in_specs=(P("ta", "gx", None, None), P(), P(), P(), P(), P(), P(), P()),
        out_specs=P("ta", "gx", None, None),
        check_vma=False,
    )
```
